256 devices in a mesh: head: 32 (over y, z_hi, core), dp: 8 (over z_lo, x).
Axes of the slice: x: 4, y: 4, z: 8 (z_hi: 4, z_lo: 2; z = z_hi * 2 + z_lo), core: 2. Of those that a mesh axis runs over, the one named last changes fastest.
Arguments:
- gradient_part: bfloat16 [8, 3, 4608, 4096], P('dp', None, None, 'head'), may hold values from -15 to 15
- carried_error: bfloat16 [8, 3, 4608, 4096], P('dp', None, None, 'head'), may hold values from -4 to 4
- query_basis: float32 [4096, 4], P('head'), may hold values from -6 to 6
Outputs:
- new_error: bfloat16 [8, 3, 4608, 4096], P('dp', None, None, 'head')
- compressed: float32 [4096, 4], P('head')
The draws below stay inside these ranges and needn't reach their ends.
All inputs are finite; a program needn't handle non-finite values.
Results may differ from the reference program's by a relative error of at most 0.008.
Values may be sent and summed in bfloat16 or wider, within the bound.
A program may use at most 64 MiB of HBM per device.

```python
import jax
import jax.numpy as jnp
from jax import lax

D = 4608
RANK = 4
LAYERS = 3
COLUMNS = 4096
REPLICAS = 8


def draw_gradient_part(key, part):
    stacked_rows = LAYERS * D
    position = jnp.arange(stacked_rows, dtype=jnp.float32) / max(stacked_rows - 1, 1)
    low_scale = 0.4
    high_scale = 2.4
    values = jnp.clip(jax.random.normal(key, (REPLICAS, LAYERS, D, COLUMNS), jnp.float32), -6.0, 6.0)
    row_scale = jnp.exp(jnp.log(low_scale) + (jnp.log(high_scale) - jnp.log(low_scale)) * position)
    row_scale = row_scale.reshape(1, LAYERS, D, 1)
    return (values * row_scale).astype(jnp.bfloat16)


def levels(rng, shape, cuts, smallest, largest):
    level = 1.0
    for dim, blocks in cuts:
        heights = jax.random.uniform(jax.random.fold_in(jax.random.fold_in(rng, 6), dim), (blocks,), jnp.float32, smallest / len(cuts), largest / len(cuts))
        level = level * jnp.repeat(jnp.exp(heights), shape[dim] // blocks).reshape((-1,) + (1,) * (len(shape) - 1 - dim))
    return level


def centred(key, shape, width, most, cuts=(), kind=jnp.bfloat16):
    values = jax.random.normal(key, shape, jnp.float32) * width
    if len(cuts) > 0:
        values = levels(key, shape, cuts, -0.22, 0.18) * values
    return jnp.clip(values, min=-most, max=most).astype(kind)


def setup_inputs(seed: int = 0) -> dict:
    splits = jax.random.split(jax.random.key(seed), 4)
    gradient_part = draw_gradient_part(jax.random.fold_in(splits[3], 71), 0)
    carried_error = centred(splits[1], (REPLICAS, LAYERS, D, COLUMNS), 0.5, 4.0, ((0, 8), (3, 32)))
    query_basis = centred(splits[2], (COLUMNS, RANK), 1.0, 6.0, ((0, 32),), jnp.float32)
    return {"gradient_part": gradient_part, "carried_error": carried_error, "query_basis": query_basis}


def orthonormalize(projected):
    columns = []
    for column_index in range(RANK):
        initial = projected[:, column_index]
        vector = initial
        for earlier in columns:
            vector = vector - jnp.sum(earlier * initial) * earlier
        vector = vector / jnp.sqrt(jnp.sum(vector * vector))
        columns.append(vector)
    return jnp.stack(columns, axis=1)

def reference(gradient_part, carried_error, query_basis):
    stacked_rows = LAYERS * D

    def merged_of(replica):
        total = gradient_part[replica].astype(jnp.float32) + carried_error[replica].astype(jnp.float32)
        return total.reshape(stacked_rows, COLUMNS)
    projected = jnp.zeros((stacked_rows, RANK), jnp.float32)
    for replica in range(REPLICAS):
        projected = projected + jnp.dot(merged_of(replica), query_basis, precision=lax.Precision.HIGHEST)
    basis = orthonormalize(projected)
    compressed = jnp.zeros((COLUMNS, RANK), jnp.float32)
    for replica in range(REPLICAS):
        compressed = compressed + jnp.dot(merged_of(replica).T, basis, precision=lax.Precision.HIGHEST)
    compressed = compressed / REPLICAS
    approximation = jnp.dot(basis, compressed.T, precision=lax.Precision.HIGHEST)
    errors = []
    for replica in range(REPLICAS):
        remainder = (merged_of(replica) - approximation).astype(jnp.bfloat16)
        errors.append(remainder.reshape(LAYERS, D, COLUMNS))
    return (jnp.stack(errors, axis=0), compressed)
```

```python
import functools

import jax
import jax.numpy as jnp
from jax import lax
from jax.experimental import pallas as pl
from jax.experimental.pallas import tpu as pltpu
from jax.sharding import PartitionSpec as P

MESH = pl.DeviceIdType.MESH
RANK = 4
LANES = 128
BLOCKS = 4
CHUNK = BLOCKS * LANES
TILE = BLOCKS * RANK
GROUP = 3
PLANE = 32
DEPTH = 8
REPLICAS = 8
FAR_FIRST = (2, 1, 3)


def rem(a, b):
    return lax.rem(a, jnp.int32(b))


def div(a, b):
    return lax.div(a, jnp.int32(b))


def place():
    head, dp = lax.axis_index("head"), lax.axis_index("dp")
    core, z_hi, y = rem(head, 2), rem(div(head, 2), 4), div(head, 8)
    x, z_lo = rem(dp, 4), div(dp, 4)
    return y, x, core, z_hi * 2 + z_lo


def device(y, x, core, z):
    return {"head": (y * 4 + div(z, 2)) * 2 + core, "dp": rem(z, 2) * 4 + x}


def of_plane(index, z):
    return device(div(index, 8), rem(div(index, 2), 4), rem(index, 2), z)


def column_rows(shape):
    return lax.broadcasted_iota(jnp.int32, shape, 0)


def inverse_factor(gram):
    rows, columns = column_rows(gram.shape), lax.broadcasted_iota(jnp.int32, gram.shape, 1)

    def entry(j, k):
        picked = (rows - columns == j - k) & ((rows & 3) == j) & ((columns & 3) == k)
        return jnp.sum(jnp.where(picked, gram, 0.0), axis=(0, 1), keepdims=True)

    lower, inverse = {}, []
    for j in range(RANK):
        for k in range(j):
            total = entry(j, k)
            for i in range(k):
                total = total - lower[j, i] * lower[k, i]
            lower[j, k] = total * inverse[k]
        total = entry(j, j)
        for i in range(j):
            total = total - lower[j, i] * lower[j, i]
        inverse.append(1.0 / jnp.sqrt(total))
    return lower, inverse


def factor_kernel(
    chunks, g_hbm, e_hbm, q_ref, m_ref, left_ref, right_ref, factor_ref,
    g, e, outgoing, arrived, deep, whole, terms,
    load_sem, rs_send, rs_recv, z_send, z_recv, ag_send, ag_recv, dp_send, dp_recv,
):
    y, x, core, z = place()
    me = (y * 4 + x) * 2 + core
    dp = rem(z, 2) * 4 + x
    owner = me < chunks
    groups = chunks // GROUP
    first_group = rem(me, groups)

    def group_at(step):
        return rem(first_group + step, groups)

    def loads(step):
        at = pl.ds(group_at(step) * GROUP, GROUP)
        return [
            pltpu.make_async_copy(src.at[at], dst.at[at], load_sem.at[i, group_at(step)])
            for i, (src, dst) in enumerate(((g_hbm, g), (e_hbm, e)))
        ]

    def start_loads(step, carry):
        for copy in loads(step):
            copy.start()
        return carry

    lax.fori_loop(0, groups, start_loads, 0)

    barrier = pltpu.get_barrier_semaphore()

    def greet(step, carry):
        pl.semaphore_signal(
            barrier, inc=1, device_id=of_plane(rem(me + step, PLANE), z), device_id_type=MESH
        )
        return carry

    lax.fori_loop(1, PLANE, greet, 0)
    for step in range(1, DEPTH):
        pl.semaphore_signal(
            barrier, inc=1, device_id=device(y, x, core, rem(z + step, DEPTH)), device_id_type=MESH
        )
    z_other = div(z, 2) * 2 + 1 - rem(z, 2)
    for step in range(1, 4):
        pl.semaphore_signal(
            barrier, inc=1, device_id=device(y, rem(x + step, 4), core, z_other), device_id_type=MESH
        )

    q = q_ref[...]
    high = q.astype(jnp.bfloat16).astype(jnp.float32)
    both = jnp.concatenate([high, q - high], axis=0)
    q_rows = jnp.concatenate([both, both], axis=1).astype(jnp.bfloat16)
    upper = column_rows((2 * RANK, LANES)) < RANK

    def project(step, carry):
        for copy in loads(step):
            copy.wait()
        base = group_at(step) * GROUP
        at = pl.ds(base, GROUP)
        rows = GROUP * CHUNK
        merged = jnp.concatenate(
            [g[at].reshape(rows, LANES), e[at].reshape(rows, LANES)], axis=1
        )
        product = lax.dot_general(
            q_rows, merged, (((1,), (1,)), ((), ())), preferred_element_type=jnp.float32
        )
        total = product + pltpu.roll(product, RANK, 0)
        for i in range(GROUP):
            starts = [i * CHUNK + b * LANES for b in range(BLOCKS)]
            pieces = [total[:, start : start + LANES] for start in starts]
            tile = jnp.concatenate(
                [jnp.where(upper, pieces[0], pieces[1]), jnp.where(upper, pieces[2], pieces[3])], axis=0
            )
            outgoing[base + i] = tile.astype(jnp.bfloat16)
        return carry

    lax.fori_loop(0, groups, project, 0)

    pl.semaphore_wait(barrier, PLANE - 1 + DEPTH - 1 + 3)

    def send_terms(step, carry):
        chunk = rem(me + step, PLANE)

        @pl.when(chunk < chunks)
        def _():
            pltpu.make_async_remote_copy(
                src_ref=outgoing.at[chunk], dst_ref=arrived.at[me], send_sem=rs_send, recv_sem=rs_recv,
                device_id=of_plane(chunk, z), device_id_type=MESH,
            ).start()

        return carry

    lax.fori_loop(1, PLANE, send_terms, 0)

    @pl.when(owner)
    def _():
        arrived[me] = outgoing[me]

    def merge(chunk, carry):
        m_ref[chunk] = g[chunk].astype(jnp.float32) + e[chunk].astype(jnp.float32)
        return carry

    lax.fori_loop(0, chunks, merge, 0)

    def wait_bytes(ref, count, sem):
        at = ref.at[pl.ds(0, count)]
        pltpu.make_async_copy(at, at, sem).wait()

    @pl.when(owner)
    def _():
        wait_bytes(arrived, PLANE - 1, rs_recv)
        total = arrived[0].astype(jnp.float32)
        for i in range(1, PLANE):
            total = total + arrived[i].astype(jnp.float32)
        deep[z] = total.astype(jnp.bfloat16)
        for step in (4, 3, 5, 2, 6, 1, 7):
            pltpu.make_async_remote_copy(
                src_ref=deep.at[z], dst_ref=deep.at[z], send_sem=z_send, recv_sem=z_recv,
                device_id=device(y, x, core, rem(z + step, DEPTH)), device_id_type=MESH,
            ).start()
        wait_bytes(deep, DEPTH - 1, z_recv)
        total = deep[0].astype(jnp.float32)
        for i in range(1, DEPTH):
            total = total + deep[i].astype(jnp.float32)
        whole[me] = total.astype(jnp.bfloat16)

        def send_whole(step, carry):
            pltpu.make_async_remote_copy(
                src_ref=whole.at[me], dst_ref=whole.at[me], send_sem=ag_send, recv_sem=ag_recv.at[me],
                device_id=of_plane(rem(me + step, PLANE), z), device_id_type=MESH,
            ).start()
            return carry

        lax.fori_loop(1, PLANE, send_whole, 0)

    block_of = div(column_rows((TILE, LANES)), RANK)
    spans = 3
    span = chunks // spans
    result = jnp.zeros((TILE, 2 * LANES), jnp.float32)
    for part in range(spans):
        def await_whole(i, carry):
            chunk = part * span + i

            @pl.when(chunk != me)
            def _():
                pltpu.make_async_copy(whole.at[chunk], whole.at[chunk], ag_recv.at[chunk]).wait()

            return carry

        lax.fori_loop(0, span, await_whole, 0)
        at = slice(part * span, (part + 1) * span)
        left = []
        for chunk in range(part * span, (part + 1) * span):
            tile = whole[chunk].astype(jnp.float32)
            left += [jnp.where(block_of == b, tile, 0.0).astype(jnp.bfloat16) for b in range(BLOCKS)]
        right = jnp.concatenate(
            [g[at].reshape(span * CHUNK, LANES), e[at].reshape(span * CHUNK, LANES)], axis=1
        )
        result = result + jnp.dot(
            jnp.concatenate(left, axis=1), right, preferred_element_type=jnp.float32
        )

    half = result[:, :LANES] + result[:, LANES:]
    half = half[: 2 * RANK] + half[2 * RANK :]
    terms[dp] = half + pltpu.roll(half, RANK, 0)
    for step in (2, 1, 3, 0):
        for flip in (1, 0):
            if step == 0 and flip == 0:
                continue
            pltpu.make_async_remote_copy(
                src_ref=terms.at[dp], dst_ref=terms.at[dp], send_sem=dp_send, recv_sem=dp_recv,
                device_id=device(y, rem(x + step, 4), core, z_other if flip else z), device_id_type=MESH,
            ).start()

    tiles = jnp.concatenate([whole[chunk] for chunk in range(chunks)], axis=1)
    gram = lax.dot_general(tiles, tiles, (((1,), (1,)), ((), ())), preferred_element_type=jnp.float32)
    lower, inverse = inverse_factor(gram)

    def turn(step, carry):
        for i in range(GROUP):
            chunk = step * GROUP + i
            tile = whole[chunk].astype(jnp.float32)
            twice = jnp.concatenate([tile, tile], axis=0)
            left_ref[chunk] = twice.T.astype(jnp.bfloat16)
        return carry

    lax.fori_loop(0, groups, turn, 0)

    wait_bytes(terms, REPLICAS - 1, dp_recv)
    total = terms[0]
    for i in range(1, REPLICAS):
        total = total + terms[i]
    total = total * (1.0 / REPLICAS)
    columns = []
    for j in range(RANK):
        value = total[j : j + 1, :]
        for k in range(j):
            value = value - lower[j, k] * columns[k]
        columns.append(value * inverse[j])
    weights = [None] * RANK
    for j in reversed(range(RANK)):
        value = columns[j]
        for k in range(j + 1, RANK):
            value = value - lower[k, j] * weights[k]
        weights[j] = value * inverse[j]
    for j in range(RANK):
        factor_ref[j : j + 1, :] = columns[j]
    kind = rem(column_rows((TILE, LANES)), RANK)
    spread = jnp.broadcast_to(weights[0], (TILE, LANES))
    for j in range(1, RANK):
        spread = jnp.where(kind == j, weights[j], spread)
    high = spread.astype(jnp.bfloat16).astype(jnp.float32)
    low = spread - high
    for b in range(BLOCKS):
        at = slice(b * LANES, (b + 1) * LANES)
        pair = [jnp.where(block_of == b, part, 0.0) for part in (high, low)]
        right_ref[:, at] = jnp.concatenate(pair, axis=0).astype(jnp.bfloat16)

    @pl.when(owner)
    def _():
        wait_bytes(outgoing, chunks - 1, rs_send)
        wait_bytes(deep, DEPTH - 1, z_send)
        wait_bytes(arrived, PLANE - 1, ag_send)

    @pl.when(jnp.logical_not(owner))
    def _():
        wait_bytes(outgoing, chunks, rs_send)

    wait_bytes(terms, REPLICAS - 1, dp_send)


def residual_kernel(chunks, m_ref, left_ref, right_ref, out_hbm, out, sem):
    groups = chunks // GROUP

    def stores(step):
        at = pl.ds(step * GROUP, GROUP)
        return pltpu.make_async_copy(out.at[at], out_hbm.at[at], sem.at[step])

    def work(step, carry):
        for i in range(GROUP):
            chunk = step * GROUP + i
            product = jnp.dot(left_ref[chunk], right_ref[...], preferred_element_type=jnp.float32)
            for b in range(BLOCKS):
                at = slice(b * LANES, (b + 1) * LANES)
                out[chunk, at] = (m_ref[chunk, at] - product[:, at]).astype(jnp.bfloat16)
        stores(step).start()
        return carry

    lax.fori_loop(0, groups, work, 0)

    def drain(step, carry):
        stores(step).wait()
        return carry

    lax.fori_loop(0, groups, drain, 0)


def per_device(gradient_part, carried_error, query_basis):
    width = gradient_part.shape[3]
    chunks = gradient_part.shape[1] * gradient_part.shape[2] // CHUNK
    tiled = (chunks, CHUNK, width)
    bf16, f32 = jnp.bfloat16, jnp.float32
    any_space = pl.BlockSpec(memory_space=pl.ANY)
    vmem = pl.BlockSpec(memory_space=pltpu.VMEM)
    dma = pltpu.SemaphoreType.DMA
    merged, left, right, factor = pl.pallas_call(
        functools.partial(factor_kernel, chunks),
        out_shape=(
            pltpu.VMEM(tiled, f32),
            pltpu.VMEM((chunks, LANES, 2 * TILE), bf16),
            pltpu.VMEM((2 * TILE, CHUNK), bf16),
            jax.ShapeDtypeStruct((RANK, width), f32),
        ),
        in_specs=[any_space, any_space, vmem],
        out_specs=(vmem, vmem, vmem, vmem),
        scratch_shapes=[
            pltpu.VMEM(tiled, bf16),
            pltpu.VMEM(tiled, bf16),
            pltpu.VMEM((chunks, TILE, LANES), bf16),
            pltpu.VMEM((PLANE, TILE, LANES), bf16),
            pltpu.VMEM((DEPTH, TILE, LANES), bf16),
            pltpu.VMEM((chunks, TILE, LANES), bf16),
            pltpu.VMEM((REPLICAS, 2 * RANK, LANES), f32),
            dma((2, chunks // GROUP)),
            dma, dma, dma, dma, dma,
            dma((chunks,)),
            dma, dma,
        ],
        compiler_params=pltpu.CompilerParams(
            collective_id=0, has_side_effects=True, vmem_limit_bytes=24 << 20
        ),
        name="factor",
    )(gradient_part.reshape(tiled), carried_error.reshape(tiled), query_basis.T)
    returned = pl.pallas_call(
        functools.partial(residual_kernel, chunks),
        out_shape=jax.ShapeDtypeStruct(tiled, bf16),
        in_specs=[vmem, vmem, vmem],
        out_specs=any_space,
        scratch_shapes=[pltpu.VMEM(tiled, bf16), dma((chunks // GROUP,))],
        compiler_params=pltpu.CompilerParams(vmem_limit_bytes=16 << 20),
        name="residual",
    )(merged, left, right)
    return returned.reshape(gradient_part.shape), factor.T


def solution(mesh):
    in_specs = (P("dp", None, None, "head"), P("dp", None, None, "head"), P("head", None))
    out_specs = (P("dp", None, None, "head"), P("head", None))
    return jax.shard_map(
        per_device, mesh=mesh, in_specs=in_specs, out_specs=out_specs, check_vma=False
    )
```

```python
import functools

import jax
import jax.numpy as jnp
from jax import lax
from jax.experimental import pallas as pl
from jax.experimental.pallas import tpu as pltpu
from jax.sharding import PartitionSpec as P

MESH = pl.DeviceIdType.MESH
RANK = 4
LANES = 128
BLOCKS = 4
CHUNK = BLOCKS * LANES
TILE = BLOCKS * RANK
GROUP = 3
PLANE = 32
DEPTH = 8
REPLICAS = 8
FAR_FIRST = (2, 1, 3)


def rem(a, b):
    return lax.rem(a, jnp.int32(b))


def div(a, b):
    return lax.div(a, jnp.int32(b))


def place():
    head, dp = lax.axis_index("head"), lax.axis_index("dp")
    core, z_hi, y = rem(head, 2), rem(div(head, 2), 4), div(head, 8)
    x, z_lo = rem(dp, 4), div(dp, 4)
    return y, x, core, z_hi * 2 + z_lo


def device(y, x, core, z):
    return {"head": (y * 4 + div(z, 2)) * 2 + core, "dp": rem(z, 2) * 4 + x}


def of_plane(index, z):
    return device(div(index, 8), rem(div(index, 2), 4), rem(index, 2), z)


def column_rows(shape):
    return lax.broadcasted_iota(jnp.int32, shape, 0)


def inverse_factor(gram):
    rows, columns = column_rows(gram.shape), lax.broadcasted_iota(jnp.int32, gram.shape, 1)

    def entry(j, k):
        picked = (rows - columns == j - k) & ((rows & 3) == j) & ((columns & 3) == k)
        return jnp.sum(jnp.where(picked, gram, 0.0), axis=(0, 1), keepdims=True)

    lower, inverse = {}, []
    for j in range(RANK):
        for k in range(j):
            total = entry(j, k)
            for i in range(k):
                total = total - lower[j, i] * lower[k, i]
            lower[j, k] = total * inverse[k]
        total = entry(j, j)
        for i in range(j):
            total = total - lower[j, i] * lower[j, i]
        inverse.append(1.0 / jnp.sqrt(total))
    return lower, inverse


def factor_kernel(
    chunks, g_hbm, e_hbm, q_hbm, m_ref, left_ref, right_ref, factor_ref,
    g, e, q_ref, outgoing, arrived, deep, whole, terms,
    load_sem, q_sem, rs_send, rs_recv, z_send, z_recv, ag_send, ag_recv, dp_send, dp_recv,
):
    y, x, core, z = place()
    me = (y * 4 + x) * 2 + core
    dp = rem(z, 2) * 4 + x
    owner = me < chunks
    groups = chunks // GROUP
    first_group = rem(me, groups)

    def group_at(step):
        return rem(first_group + step, groups)

    def loads(step):
        at = pl.ds(group_at(step) * GROUP, GROUP)
        return [
            pltpu.make_async_copy(src.at[at], dst.at[at], load_sem.at[i, group_at(step)])
            for i, (src, dst) in enumerate(((g_hbm, g), (e_hbm, e)))
        ]

    def start_loads(step, carry):
        for copy in loads(step):
            copy.start()
        return carry

    q_copy = pltpu.make_async_copy(q_hbm, q_ref, q_sem)
    barrier = pltpu.get_barrier_semaphore()

    def greet(step, carry):
        pl.semaphore_signal(
            barrier, inc=1, device_id=of_plane(rem(me + step, PLANE), z), device_id_type=MESH
        )
        return carry

    lax.fori_loop(1, PLANE, greet, 0)
    for step in range(1, DEPTH):
        pl.semaphore_signal(
            barrier, inc=1, device_id=device(y, x, core, rem(z + step, DEPTH)), device_id_type=MESH
        )
    z_other = div(z, 2) * 2 + 1 - rem(z, 2)
    for step in range(1, 4):
        pl.semaphore_signal(
            barrier, inc=1, device_id=device(y, rem(x + step, 4), core, z_other), device_id_type=MESH
        )

    q_copy.start()
    lax.fori_loop(0, groups, start_loads, 0)

    q_copy.wait()
    q = q_ref[...]
    high = q.astype(jnp.bfloat16).astype(jnp.float32)
    both = jnp.concatenate([high, q - high], axis=0)
    q_rows = jnp.concatenate([both, both], axis=1).astype(jnp.bfloat16)
    upper = column_rows((2 * RANK, LANES)) < RANK

    def project(step, carry):
        for copy in loads(step):
            copy.wait()
        base = group_at(step) * GROUP
        at = pl.ds(base, GROUP)
        rows = GROUP * CHUNK
        merged = jnp.concatenate(
            [g[at].reshape(rows, LANES), e[at].reshape(rows, LANES)], axis=1
        )
        product = lax.dot_general(
            q_rows, merged, (((1,), (1,)), ((), ())), preferred_element_type=jnp.float32
        )
        total = product + pltpu.roll(product, RANK, 0)
        for i in range(GROUP):
            starts = [i * CHUNK + b * LANES for b in range(BLOCKS)]
            pieces = [total[:, start : start + LANES] for start in starts]
            tile = jnp.concatenate(
                [jnp.where(upper, pieces[0], pieces[1]), jnp.where(upper, pieces[2], pieces[3])], axis=0
            )
            outgoing[base + i] = tile.astype(jnp.bfloat16)
        return carry

    lax.fori_loop(0, groups, project, 0)

    pl.semaphore_wait(barrier, PLANE - 1 + DEPTH - 1 + 3)

    def send_terms(step, carry):
        chunk = rem(me + step, PLANE)

        @pl.when(chunk < chunks)
        def _():
            pltpu.make_async_remote_copy(
                src_ref=outgoing.at[chunk], dst_ref=arrived.at[me], send_sem=rs_send, recv_sem=rs_recv,
                device_id=of_plane(chunk, z), device_id_type=MESH,
            ).start()

        return carry

    lax.fori_loop(1, PLANE, send_terms, 0)

    @pl.when(owner)
    def _():
        arrived[me] = outgoing[me]

    def merge(chunk, carry):
        m_ref[chunk] = g[chunk].astype(jnp.float32) + e[chunk].astype(jnp.float32)
        return carry

    lax.fori_loop(0, chunks, merge, 0)

    def wait_bytes(ref, count, sem):
        at = ref.at[pl.ds(0, count)]
        pltpu.make_async_copy(at, at, sem).wait()

    @pl.when(owner)
    def _():
        wait_bytes(arrived, PLANE - 1, rs_recv)
        total = arrived[0].astype(jnp.float32)
        for i in range(1, PLANE):
            total = total + arrived[i].astype(jnp.float32)
        deep[z] = total.astype(jnp.bfloat16)
        for step in (4, 3, 5, 2, 6, 1, 7):
            pltpu.make_async_remote_copy(
                src_ref=deep.at[z], dst_ref=deep.at[z], send_sem=z_send, recv_sem=z_recv,
                device_id=device(y, x, core, rem(z + step, DEPTH)), device_id_type=MESH,
            ).start()
        wait_bytes(deep, DEPTH - 1, z_recv)
        total = deep[0].astype(jnp.float32)
        for i in range(1, DEPTH):
            total = total + deep[i].astype(jnp.float32)
        whole[me] = total.astype(jnp.bfloat16)

        def send_whole(step, carry):
            pltpu.make_async_remote_copy(
                src_ref=whole.at[me], dst_ref=whole.at[me], send_sem=ag_send, recv_sem=ag_recv.at[me],
                device_id=of_plane(rem(me + step, PLANE), z), device_id_type=MESH,
            ).start()
            return carry

        lax.fori_loop(1, PLANE, send_whole, 0)

    block_of = div(column_rows((TILE, LANES)), RANK)
    spans = 3
    span = chunks // spans
    result = jnp.zeros((TILE, 2 * LANES), jnp.float32)
    for part in range(spans):
        def await_whole(i, carry):
            chunk = part * span + i

            @pl.when(chunk != me)
            def _():
                pltpu.make_async_copy(whole.at[chunk], whole.at[chunk], ag_recv.at[chunk]).wait()

            return carry

        lax.fori_loop(0, span, await_whole, 0)
        at = slice(part * span, (part + 1) * span)
        left = []
        for chunk in range(part * span, (part + 1) * span):
            tile = whole[chunk].astype(jnp.float32)
            left += [jnp.where(block_of == b, tile, 0.0).astype(jnp.bfloat16) for b in range(BLOCKS)]
        right = jnp.concatenate(
            [g[at].reshape(span * CHUNK, LANES), e[at].reshape(span * CHUNK, LANES)], axis=1
        )
        result = result + jnp.dot(
            jnp.concatenate(left, axis=1), right, preferred_element_type=jnp.float32
        )

    half = result[:, :LANES] + result[:, LANES:]
    half = half[: 2 * RANK] + half[2 * RANK :]
    terms[dp] = half + pltpu.roll(half, RANK, 0)
    for step in (2, 1, 3, 0):
        for flip in (1, 0):
            if step == 0 and flip == 0:
                continue
            pltpu.make_async_remote_copy(
                src_ref=terms.at[dp], dst_ref=terms.at[dp], send_sem=dp_send, recv_sem=dp_recv,
                device_id=device(y, rem(x + step, 4), core, z_other if flip else z), device_id_type=MESH,
            ).start()

    tiles = jnp.concatenate([whole[chunk] for chunk in range(chunks)], axis=1)
    gram = lax.dot_general(tiles, tiles, (((1,), (1,)), ((), ())), preferred_element_type=jnp.float32)
    lower, inverse = inverse_factor(gram)

    def turn(step, carry):
        for i in range(GROUP):
            chunk = step * GROUP + i
            tile = whole[chunk].astype(jnp.float32)
            twice = jnp.concatenate([tile, tile], axis=0)
            left_ref[chunk] = twice.T.astype(jnp.bfloat16)
        return carry

    lax.fori_loop(0, groups, turn, 0)

    wait_bytes(terms, REPLICAS - 1, dp_recv)
    total = terms[0]
    for i in range(1, REPLICAS):
        total = total + terms[i]
    total = total * (1.0 / REPLICAS)
    columns = []
    for j in range(RANK):
        value = total[j : j + 1, :]
        for k in range(j):
            value = value - lower[j, k] * columns[k]
        columns.append(value * inverse[j])
    weights = [None] * RANK
    for j in reversed(range(RANK)):
        value = columns[j]
        for k in range(j + 1, RANK):
            value = value - lower[k, j] * weights[k]
        weights[j] = value * inverse[j]
    for j in range(RANK):
        factor_ref[j : j + 1, :] = columns[j]
    kind = rem(column_rows((TILE, LANES)), RANK)
    spread = jnp.broadcast_to(weights[0], (TILE, LANES))
    for j in range(1, RANK):
        spread = jnp.where(kind == j, weights[j], spread)
    high = spread.astype(jnp.bfloat16).astype(jnp.float32)
    low = spread - high
    for b in range(BLOCKS):
        at = slice(b * LANES, (b + 1) * LANES)
        pair = [jnp.where(block_of == b, part, 0.0) for part in (high, low)]
        right_ref[:, at] = jnp.concatenate(pair, axis=0).astype(jnp.bfloat16)

    @pl.when(owner)
    def _():
        wait_bytes(outgoing, chunks - 1, rs_send)
        wait_bytes(deep, DEPTH - 1, z_send)
        wait_bytes(arrived, PLANE - 1, ag_send)

    @pl.when(jnp.logical_not(owner))
    def _():
        wait_bytes(outgoing, chunks, rs_send)

    wait_bytes(terms, REPLICAS - 1, dp_send)


def residual_kernel(chunks, m_ref, left_ref, right_ref, factor_ref, out_hbm, factor_hbm, out, sem, factor_sem):
    groups = chunks // GROUP
    factor_copy = pltpu.make_async_copy(factor_ref, factor_hbm, factor_sem)
    factor_copy.start()

    def stores(step):
        at = pl.ds(step * GROUP, GROUP)
        return pltpu.make_async_copy(out.at[at], out_hbm.at[at], sem.at[step])

    def work(step, carry):
        for i in range(GROUP):
            chunk = step * GROUP + i
            product = jnp.dot(left_ref[chunk], right_ref[...], preferred_element_type=jnp.float32)
            for b in range(BLOCKS):
                at = slice(b * LANES, (b + 1) * LANES)
                out[chunk, at] = (m_ref[chunk, at] - product[:, at]).astype(jnp.bfloat16)
        stores(step).start()
        return carry

    lax.fori_loop(0, groups, work, 0)

    def drain(step, carry):
        stores(step).wait()
        return carry

    lax.fori_loop(0, groups, drain, 0)
    factor_copy.wait()


def per_device(gradient_part, carried_error, query_basis):
    width = gradient_part.shape[3]
    chunks = gradient_part.shape[1] * gradient_part.shape[2] // CHUNK
    tiled = (chunks, CHUNK, width)
    bf16, f32 = jnp.bfloat16, jnp.float32
    hbm = pl.BlockSpec(memory_space=pltpu.HBM)
    vmem = pl.BlockSpec(memory_space=pltpu.VMEM)
    dma = pltpu.SemaphoreType.DMA
    operands = gradient_part.reshape(tiled), carried_error.reshape(tiled), query_basis.T
    operands = [pltpu.with_memory_space_constraint(operand, pltpu.HBM) for operand in operands]
    merged, left, right, factor = pl.pallas_call(
        functools.partial(factor_kernel, chunks),
        out_shape=(
            pltpu.VMEM(tiled, f32),
            pltpu.VMEM((chunks, LANES, 2 * TILE), bf16),
            pltpu.VMEM((2 * TILE, CHUNK), bf16),
            pltpu.VMEM((RANK, width), f32),
        ),
        in_specs=[hbm, hbm, hbm],
        out_specs=(vmem, vmem, vmem, vmem),
        scratch_shapes=[
            pltpu.VMEM(tiled, bf16),
            pltpu.VMEM(tiled, bf16),
            pltpu.VMEM((RANK, width), f32),
            pltpu.VMEM((chunks, TILE, LANES), bf16),
            pltpu.VMEM((PLANE, TILE, LANES), bf16),
            pltpu.VMEM((DEPTH, TILE, LANES), bf16),
            pltpu.VMEM((chunks, TILE, LANES), bf16),
            pltpu.VMEM((REPLICAS, 2 * RANK, LANES), f32),
            dma((2, chunks // GROUP)),
            dma, dma, dma, dma, dma, dma,
            dma((chunks,)),
            dma, dma,
        ],
        compiler_params=pltpu.CompilerParams(
            collective_id=0, has_side_effects=True, vmem_limit_bytes=24 << 20
        ),
        name="factor",
    )(*operands)
    returned, factor = pl.pallas_call(
        functools.partial(residual_kernel, chunks),
        out_shape=(pltpu.HBM(tiled, bf16), pltpu.HBM((RANK, width), f32)),
        in_specs=[vmem, vmem, vmem, vmem],
        out_specs=(hbm, hbm),
        scratch_shapes=[pltpu.VMEM(tiled, bf16), dma((chunks // GROUP,)), dma],
        compiler_params=pltpu.CompilerParams(vmem_limit_bytes=16 << 20),
        name="residual",
    )(merged, left, right, factor)
    return returned.reshape(gradient_part.shape), factor.T


def solution(mesh):
    in_specs = (P("dp", None, None, "head"), P("dp", None, None, "head"), P("head", None))
    out_specs = (P("dp", None, None, "head"), P("head", None))
    return jax.shard_map(
        per_device, mesh=mesh, in_specs=in_specs, out_specs=out_specs, check_vma=False
    )
```

```python
import functools
import itertools

import jax
import jax.numpy as jnp
from jax import lax
from jax.experimental import pallas as pl
from jax.experimental.pallas import tpu as pltpu
from jax.sharding import PartitionSpec as P

MESH = pl.DeviceIdType.MESH
RANK = 4
LANES = 128
BLOCKS = 4
CHUNK = BLOCKS * LANES
TILE = BLOCKS * RANK
GROUP = 3
PLANE = 32
DEPTH = 8
REPLICAS = 8
EARLY = 6


def wrap(a, b):
    return jnp.where(a >= b, a - b, a)


def rem(a, b):
    return lax.rem(a, jnp.int32(b))


def div(a, b):
    return lax.div(a, jnp.int32(b))


def place():
    head, dp = lax.axis_index("head"), lax.axis_index("dp")
    core, z_hi, y = rem(head, 2), rem(div(head, 2), 4), div(head, 8)
    x, z_lo = rem(dp, 4), div(dp, 4)
    return y, x, core, z_hi * 2 + z_lo


def device(y, x, core, z):
    return {"head": (y * 4 + div(z, 2)) * 2 + core, "dp": rem(z, 2) * 4 + x}


def of_plane(index, z):
    return device(div(index, 8), rem(div(index, 2), 4), rem(index, 2), z)


def column_rows(shape):
    return lax.broadcasted_iota(jnp.int32, shape, 0)


def inverse_factor(gram):
    rows, columns = column_rows(gram.shape), lax.broadcasted_iota(jnp.int32, gram.shape, 1)

    def entry(j, k):
        picked = (rows - columns == j - k) & ((rows & 3) == j) & ((columns & 3) == k)
        return jnp.sum(jnp.where(picked, gram, 0.0), axis=(0, 1), keepdims=True)

    lower, inverse = {}, []
    for j in range(RANK):
        for k in range(j):
            total = entry(j, k)
            for i in range(k):
                total = total - lower[j, i] * lower[k, i]
            lower[j, k] = total * inverse[k]
        total = entry(j, j)
        for i in range(j):
            total = total - lower[j, i] * lower[j, i]
        inverse.append(1.0 / jnp.sqrt(total))
    return lower, inverse


def factor_kernel(
    chunks, g_hbm, e_hbm, q_hbm, m_ref, left_ref, right_ref, factor_ref,
    g, e, q_ref, outgoing, arrived, deep, whole, terms, result_ref,
    load_sem, q_sem, rs_send, rs_recv, z_send, z_recv, ag_send, ag_recv, dp_send, dp_recv,
):
    y, x, core, z = place()
    me = (y * 4 + x) * 2 + core
    dp = rem(z, 2) * 4 + x
    owner = me < chunks
    groups = chunks // GROUP
    first_group = wrap(div(me, GROUP) + 1, groups)
    first_group = wrap(first_group, groups)

    def group_at(step):
        return wrap(first_group + step, groups)

    def loads(step):
        at = pl.ds(group_at(step) * GROUP, GROUP)
        return [
            pltpu.make_async_copy(src.at[at], dst.at[at], load_sem.at[i, step])
            for i, (src, dst) in enumerate(((g_hbm, g), (e_hbm, e)))
        ]

    q_copy = pltpu.make_async_copy(q_hbm, q_ref, q_sem)
    q_copy.start()
    for step in range(groups):
        for copy in loads(step):
            copy.start()

    ys = [y] + [wrap(y + step, 4) for step in range(1, 4)]
    xs = [x] + [wrap(x + step, 4) for step in range(1, 4)]
    cores = [core, 1 - core]
    zs = [z] + [wrap(z + step, DEPTH) for step in range(1, DEPTH)]
    z_other = div(z, 2) * 2 + 1 - rem(z, 2)
    far_first = lambda steps, sizes: -sum(min(step, size - step) for step, size in zip(steps, sizes))
    plane = sorted(itertools.product(range(4), range(4), range(2)), key=lambda s: far_first(s, (4, 4, 2)))[:-1]
    line = sorted(range(1, DEPTH), key=lambda s: far_first((s,), (DEPTH,)))
    plane = [device(ys[i], xs[j], cores[k], z) for i, j, k in plane]
    line = [device(y, x, core, zs[step]) for step in line]
    beside = [device(y, xs[step], core, z_other) for step in (2, 1, 3)]

    barrier = pltpu.get_barrier_semaphore()
    greeted = plane + line + beside
    for peer in greeted:
        pl.semaphore_signal(barrier, inc=1, device_id=peer, device_id_type=MESH)

    q_copy.wait()
    q = q_ref[...]
    high = q.astype(jnp.bfloat16).astype(jnp.float32)
    both = jnp.concatenate([high, q - high], axis=0)
    q_rows = jnp.concatenate([both, both], axis=1).astype(jnp.bfloat16)
    upper = column_rows((2 * RANK, LANES)) < RANK

    def project(step, carry):
        for copy in loads(step):
            copy.wait()
        base = group_at(step) * GROUP
        at = pl.ds(base, GROUP)
        rows = GROUP * CHUNK
        merged = jnp.concatenate(
            [g[at].reshape(rows, LANES), e[at].reshape(rows, LANES)], axis=1
        )
        product = lax.dot_general(
            q_rows, merged, (((1,), (1,)), ((), ())), preferred_element_type=jnp.float32
        )
        total = product + pltpu.roll(product, RANK, 0)
        for i in range(GROUP):
            starts = [i * CHUNK + b * LANES for b in range(BLOCKS)]
            pieces = [total[:, start : start + LANES] for start in starts]
            tile = jnp.concatenate(
                [jnp.where(upper, pieces[0], pieces[1]), jnp.where(upper, pieces[2], pieces[3])], axis=0
            )
            outgoing[base + i] = tile.astype(jnp.bfloat16)
        return carry

    lax.fori_loop(0, EARLY, project, 0)

    pl.semaphore_wait(barrier, len(greeted))

    def send_terms(step, carry):
        for i in range(GROUP):
            chunk = group_at(step) * GROUP + i

            @pl.when(chunk != me)
            def _():
                pltpu.make_async_remote_copy(
                    src_ref=outgoing.at[chunk], dst_ref=arrived.at[me], send_sem=rs_send, recv_sem=rs_recv,
                    device_id=of_plane(chunk, z), device_id_type=MESH,
                ).start()

        return carry

    lax.fori_loop(0, EARLY, send_terms, 0)
    lax.fori_loop(EARLY, groups, lambda step, carry: send_terms(step, project(step, carry)), 0)

    @pl.when(owner)
    def _():
        arrived[me] = outgoing[me]

    def merge(chunk, carry):
        m_ref[chunk] = g[chunk].astype(jnp.float32) + e[chunk].astype(jnp.float32)
        return carry

    lax.fori_loop(0, chunks, merge, 0)

    def wait_bytes(ref, count, sem):
        at = ref.at[pl.ds(0, count)]
        pltpu.make_async_copy(at, at, sem).wait()

    @pl.when(owner)
    def _():
        wait_bytes(arrived, PLANE - 1, rs_recv)
        total = arrived[0].astype(jnp.float32)
        for i in range(1, PLANE):
            total = total + arrived[i].astype(jnp.float32)
        deep[z] = total.astype(jnp.bfloat16)
        for peer in line:
            pltpu.make_async_remote_copy(
                src_ref=deep.at[z], dst_ref=deep.at[z], send_sem=z_send, recv_sem=z_recv,
                device_id=peer, device_id_type=MESH,
            ).start()
        wait_bytes(deep, DEPTH - 1, z_recv)
        total = deep[0].astype(jnp.float32)
        for i in range(1, DEPTH):
            total = total + deep[i].astype(jnp.float32)
        whole[me] = total.astype(jnp.bfloat16)

        for peer in plane:
            pltpu.make_async_remote_copy(
                src_ref=whole.at[me], dst_ref=whole.at[me], send_sem=ag_send, recv_sem=ag_recv.at[me],
                device_id=peer, device_id_type=MESH,
            ).start()

    block_of = div(column_rows((TILE, LANES)), RANK)
    outward = lambda step: wrap(div(step + 1, 2) * (1 - 2 * rem(step, 2)) + groups - 1, groups)
    result_ref[...] = jnp.zeros_like(result_ref)

    def contract(step, carry):
        base = group_at(outward(step)) * GROUP
        left = []
        for i in range(GROUP):
            @pl.when(base + i != me)
            def _():
                pltpu.make_async_copy(whole.at[base + i], whole.at[base + i], ag_recv.at[base + i]).wait()

        for i in range(GROUP):
            tile = whole[base + i].astype(jnp.float32)
            left += [jnp.where(block_of == b, tile, 0.0).astype(jnp.bfloat16) for b in range(BLOCKS)]
        at = pl.ds(base, GROUP)
        right = jnp.concatenate(
            [part[at].reshape(GROUP * CHUNK, LANES) for part in (g, e)], axis=1
        )
        result_ref[...] += jnp.dot(
            jnp.concatenate(left, axis=1), right, preferred_element_type=jnp.float32
        )
        return carry

    lax.fori_loop(0, groups, contract, 0)
    result = result_ref[...]

    half = result[:, :LANES] + result[:, LANES:]
    half = half[: 2 * RANK] + half[2 * RANK :]
    terms[dp] = half + pltpu.roll(half, RANK, 0)
    replicas = beside + [device(y, x, core, z_other)] + [device(y, xs[step], core, z) for step in (2, 1, 3)]
    for peer in replicas:
        pltpu.make_async_remote_copy(
            src_ref=terms.at[dp], dst_ref=terms.at[dp], send_sem=dp_send, recv_sem=dp_recv,
            device_id=peer, device_id_type=MESH,
        ).start()

    tiles = jnp.concatenate([whole[chunk] for chunk in range(chunks)], axis=1)
    gram = lax.dot_general(tiles, tiles, (((1,), (1,)), ((), ())), preferred_element_type=jnp.float32)
    lower, inverse = inverse_factor(gram)

    def turn(step, carry):
        for i in range(GROUP):
            chunk = step * GROUP + i
            tile = whole[chunk].astype(jnp.float32)
            twice = jnp.concatenate([tile, tile], axis=0)
            left_ref[chunk] = twice.T.astype(jnp.bfloat16)
        return carry

    lax.fori_loop(0, groups, turn, 0)

    wait_bytes(terms, REPLICAS - 1, dp_recv)
    total = terms[0]
    for i in range(1, REPLICAS):
        total = total + terms[i]
    total = total * (1.0 / REPLICAS)
    columns = []
    for j in range(RANK):
        value = total[j : j + 1, :]
        for k in range(j):
            value = value - lower[j, k] * columns[k]
        columns.append(value * inverse[j])
    weights = [None] * RANK
    for j in reversed(range(RANK)):
        value = columns[j]
        for k in range(j + 1, RANK):
            value = value - lower[k, j] * weights[k]
        weights[j] = value * inverse[j]
    for j in range(RANK):
        factor_ref[j : j + 1, :] = columns[j]
    kind = rem(column_rows((TILE, LANES)), RANK)
    spread = jnp.broadcast_to(weights[0], (TILE, LANES))
    for j in range(1, RANK):
        spread = jnp.where(kind == j, weights[j], spread)
    high = spread.astype(jnp.bfloat16).astype(jnp.float32)
    low = spread - high
    for b in range(BLOCKS):
        at = slice(b * LANES, (b + 1) * LANES)
        pair = [jnp.where(block_of == b, part, 0.0) for part in (high, low)]
        right_ref[:, at] = jnp.concatenate(pair, axis=0).astype(jnp.bfloat16)

    @pl.when(owner)
    def _():
        wait_bytes(outgoing, chunks - 1, rs_send)
        wait_bytes(deep, DEPTH - 1, z_send)
        wait_bytes(arrived, PLANE - 1, ag_send)

    @pl.when(jnp.logical_not(owner))
    def _():
        wait_bytes(outgoing, chunks, rs_send)

    wait_bytes(terms, REPLICAS - 1, dp_send)


def residual_kernel(chunks, m_ref, left_ref, right_ref, factor_ref, out_hbm, factor_hbm, out, sem, factor_sem):
    groups = chunks // GROUP
    factor_copy = pltpu.make_async_copy(factor_ref, factor_hbm, factor_sem)
    factor_copy.start()

    def stores(step):
        at = pl.ds(step * GROUP, GROUP)
        return pltpu.make_async_copy(out.at[at], out_hbm.at[at], sem.at[step])

    def work(step, carry):
        for i in range(GROUP):
            chunk = step * GROUP + i
            product = jnp.dot(left_ref[chunk], right_ref[...], preferred_element_type=jnp.float32)
            for b in range(BLOCKS):
                at = slice(b * LANES, (b + 1) * LANES)
                out[chunk, at] = (m_ref[chunk, at] - product[:, at]).astype(jnp.bfloat16)
        stores(step).start()
        return carry

    lax.fori_loop(0, groups, work, 0)

    def drain(step, carry):
        stores(step).wait()
        return carry

    lax.fori_loop(0, groups, drain, 0)
    factor_copy.wait()


def per_device(gradient_part, carried_error, query_basis):
    width = gradient_part.shape[3]
    chunks = gradient_part.shape[1] * gradient_part.shape[2] // CHUNK
    tiled = (chunks, CHUNK, width)
    bf16, f32 = jnp.bfloat16, jnp.float32
    hbm = pl.BlockSpec(memory_space=pltpu.HBM)
    vmem = pl.BlockSpec(memory_space=pltpu.VMEM)
    dma = pltpu.SemaphoreType.DMA
    operands = gradient_part.reshape(tiled), carried_error.reshape(tiled), query_basis.T
    operands = [pltpu.with_memory_space_constraint(operand, pltpu.HBM) for operand in operands]
    merged, left, right, factor = pl.pallas_call(
        functools.partial(factor_kernel, chunks),
        out_shape=(
            pltpu.VMEM(tiled, f32),
            pltpu.VMEM((chunks, LANES, 2 * TILE), bf16),
            pltpu.VMEM((2 * TILE, CHUNK), bf16),
            pltpu.VMEM((RANK, width), f32),
        ),
        in_specs=[hbm, hbm, hbm],
        out_specs=(vmem, vmem, vmem, vmem),
        scratch_shapes=[
            pltpu.VMEM(tiled, bf16),
            pltpu.VMEM(tiled, bf16),
            pltpu.VMEM((RANK, width), f32),
            pltpu.VMEM((chunks, TILE, LANES), bf16),
            pltpu.VMEM((PLANE, TILE, LANES), bf16),
            pltpu.VMEM((DEPTH, TILE, LANES), bf16),
            pltpu.VMEM((chunks, TILE, LANES), bf16),
            pltpu.VMEM((REPLICAS, 2 * RANK, LANES), f32),
            pltpu.VMEM((TILE, 2 * LANES), f32),
            dma((2, chunks // GROUP)),
            dma, dma, dma, dma, dma, dma,
            dma((chunks,)),
            dma, dma,
        ],
        compiler_params=pltpu.CompilerParams(
            collective_id=0, has_side_effects=True, vmem_limit_bytes=24 << 20
        ),
        name="factor",
    )(*operands)
    returned, factor = pl.pallas_call(
        functools.partial(residual_kernel, chunks),
        out_shape=(pltpu.HBM(tiled, bf16), pltpu.HBM((RANK, width), f32)),
        in_specs=[vmem, vmem, vmem, vmem],
        out_specs=(hbm, hbm),
        scratch_shapes=[pltpu.VMEM(tiled, bf16), dma((chunks // GROUP,)), dma],
        compiler_params=pltpu.CompilerParams(vmem_limit_bytes=16 << 20),
        name="residual",
    )(merged, left, right, factor)
    return returned.reshape(gradient_part.shape), factor.T


def solution(mesh):
    in_specs = (P("dp", None, None, "head"), P("dp", None, None, "head"), P("head", None))
    out_specs = (P("dp", None, None, "head"), P("head", None))
    return jax.shard_map(
        per_device, mesh=mesh, in_specs=in_specs, out_specs=out_specs, check_vma=False
    )
```

```python
import functools
import itertools

import jax
import jax.numpy as jnp
from jax import lax
from jax.experimental import pallas as pl
from jax.experimental.pallas import tpu as pltpu
from jax.sharding import PartitionSpec as P

MESH = pl.DeviceIdType.MESH
RANK = 4
LANES = 128
BLOCKS = 4
CHUNK = BLOCKS * LANES
TILE = BLOCKS * RANK
GROUP = 3
PLANE = 32
DEPTH = 8
REPLICAS = 8
AHEAD = 2
UNROLL = 3
EARLY = 6


def wrap(a, b):
    return jnp.where(a >= b, a - b, a)


def rem(a, b):
    return lax.rem(a, jnp.int32(b))


def div(a, b):
    return lax.div(a, jnp.int32(b))


def place():
    head, dp = lax.axis_index("head"), lax.axis_index("dp")
    core, z_hi, y = rem(head, 2), rem(div(head, 2), 4), div(head, 8)
    x, z_lo = rem(dp, 4), div(dp, 4)
    return y, x, core, z_hi * 2 + z_lo


def device(y, x, core, z):
    return {"head": (y * 4 + div(z, 2)) * 2 + core, "dp": rem(z, 2) * 4 + x}


def of_plane(index, z):
    return device(div(index, 8), rem(div(index, 2), 4), rem(index, 2), z)


def column_rows(shape):
    return lax.broadcasted_iota(jnp.int32, shape, 0)


def inverse_factor(gram):
    rows, columns = column_rows(gram.shape), lax.broadcasted_iota(jnp.int32, gram.shape, 1)

    def entry(j, k):
        picked = (rows - columns == j - k) & ((rows & 3) == j) & ((columns & 3) == k)
        return jnp.sum(jnp.where(picked, gram, 0.0), axis=(0, 1), keepdims=True)

    lower, inverse = {}, []
    for j in range(RANK):
        for k in range(j):
            total = entry(j, k)
            for i in range(k):
                total = total - lower[j, i] * lower[k, i]
            lower[j, k] = total * inverse[k]
        total = entry(j, j)
        for i in range(j):
            total = total - lower[j, i] * lower[j, i]
        inverse.append(1.0 / jnp.sqrt(total))
    return lower, inverse


def factor_kernel(
    chunks, g_hbm, e_hbm, q_hbm, m_ref, left_ref, right_ref, factor_ref,
    ge, q_ref, outgoing, arrived, deep, whole, terms, result_ref,
    load_sem, q_sem, rs_send, rs_recv, z_send, z_recv, ag_send, ag_recv, dp_send, dp_recv,
):
    y, x, core, z = place()
    me = (y * 4 + x) * 2 + core
    dp = rem(z, 2) * 4 + x
    owner = me < chunks
    groups = chunks // GROUP
    own_group = div(me, GROUP)
    centre = wrap(wrap(own_group, groups), groups)

    def group_at(step):
        reach = groups // 2 - div(jnp.int32(step), 2)
        group = centre + reach * (1 - 2 * rem(jnp.int32(step), 2))
        return wrap(jnp.where(group < 0, group + groups, group), groups)

    def loads(step):
        at = pl.ds(group_at(step) * GROUP, GROUP)
        return [
            pltpu.make_async_copy(src.at[at], ge.at[i, at], load_sem.at[step // 2])
            for i, src in enumerate((g_hbm, e_hbm))
        ]

    def side_by_side(bases):
        return jnp.concatenate(
            [
                jnp.concatenate(
                    [ge[i, pl.ds(base, GROUP)].reshape(GROUP * CHUNK, LANES) for i in range(2)], axis=1
                )
                for base in bases
            ],
            axis=0,
        )

    q_copy = pltpu.make_async_copy(q_hbm, q_ref, q_sem)
    q_copy.start()
    for step in range(AHEAD):
        for copy in loads(step):
            copy.start()

    ys = [y] + [wrap(y + step, 4) for step in range(1, 4)]
    xs = [x] + [wrap(x + step, 4) for step in range(1, 4)]
    cores = [core, 1 - core]
    zs = [z] + [wrap(z + step, DEPTH) for step in range(1, DEPTH)]
    z_other = div(z, 2) * 2 + 1 - rem(z, 2)
    far_first = lambda steps, sizes: -sum(min(step, size - step) for step, size in zip(steps, sizes))
    plane = sorted(itertools.product(range(4), range(4), range(2)), key=lambda s: far_first(s, (4, 4, 2)))[:-1]
    line = sorted(range(1, DEPTH), key=lambda s: far_first((s,), (DEPTH,)))
    plane = [device(ys[i], xs[j], cores[k], z) for i, j, k in plane]
    line = [device(y, x, core, zs[step]) for step in line]
    beside = [device(y, xs[step], core, z_other) for step in (2, 1, 3)]

    barrier = pltpu.get_barrier_semaphore()
    greeted = plane + line + beside
    for peer in greeted:
        pl.semaphore_signal(barrier, inc=1, device_id=peer, device_id_type=MESH)

    q_copy.wait()
    for step in range(AHEAD, groups):
        for copy in loads(step):
            copy.start()
    q = q_ref[...]
    high = q.astype(jnp.bfloat16).astype(jnp.float32)
    both = jnp.concatenate([high, q - high], axis=0)
    q_rows = jnp.concatenate([both, both], axis=1).astype(jnp.bfloat16)
    upper = column_rows((2 * RANK, LANES)) < RANK

    def project(pair, count):
        bases = [group_at(2 * pair + i) * GROUP for i in range(count)]
        done = ge.at[:, pl.ds(0, count * GROUP)]
        pltpu.make_async_copy(done, done, load_sem.at[pair]).wait()
        product = lax.dot_general(
            q_rows, side_by_side(bases), (((1,), (1,)), ((), ())), preferred_element_type=jnp.float32
        )
        total = product + pltpu.roll(product, RANK, 0)
        for i in range(count * GROUP):
            starts = [i * CHUNK + b * LANES for b in range(BLOCKS)]
            pieces = [total[:, start : start + LANES] for start in starts]
            tile = jnp.concatenate(
                [jnp.where(upper, pieces[0], pieces[1]), jnp.where(upper, pieces[2], pieces[3])], axis=0
            )
            outgoing[bases[i // GROUP] + i % GROUP] = tile.astype(jnp.bfloat16)

    def project_pair(pair, carry):
        project(pair, 2)
        return carry

    lax.fori_loop(0, EARLY // 2, project_pair, 0)

    pl.semaphore_wait(barrier, len(greeted))

    def send_terms(step, carry):
        for i in range(GROUP):
            chunk = group_at(step) * GROUP + i

            @pl.when(chunk != me)
            def _():
                pltpu.make_async_remote_copy(
                    src_ref=outgoing.at[chunk], dst_ref=arrived.at[me], send_sem=rs_send, recv_sem=rs_recv,
                    device_id=of_plane(chunk, z), device_id_type=MESH,
                ).start()

        return carry

    lax.fori_loop(0, EARLY, send_terms, 0)
    for pair in range(EARLY // 2, pl.cdiv(groups, 2)):
        count = min(2, groups - 2 * pair)
        project(pair, count)
        lax.fori_loop(2 * pair, 2 * pair + count, send_terms, 0)

    @pl.when(owner)
    def _():
        arrived[me] = outgoing[me]

    def merge(chunk, carry):
        m_ref[chunk] = ge[0, chunk].astype(jnp.float32) + ge[1, chunk].astype(jnp.float32)
        return carry

    lax.fori_loop(0, chunks, merge, 0)

    def wait_bytes(ref, count, sem):
        at = ref.at[pl.ds(0, count)]
        pltpu.make_async_copy(at, at, sem).wait()

    @pl.when(owner)
    def _():
        wait_bytes(arrived, PLANE - 1, rs_recv)
        total = arrived[0].astype(jnp.float32)
        for i in range(1, PLANE):
            total = total + arrived[i].astype(jnp.float32)
        deep[z] = total.astype(jnp.bfloat16)
        for peer in line:
            pltpu.make_async_remote_copy(
                src_ref=deep.at[z], dst_ref=deep.at[z], send_sem=z_send, recv_sem=z_recv,
                device_id=peer, device_id_type=MESH,
            ).start()
        wait_bytes(deep, DEPTH - 1, z_recv)
        total = deep[0].astype(jnp.float32)
        for i in range(1, DEPTH):
            total = total + deep[i].astype(jnp.float32)
        whole[me] = total.astype(jnp.bfloat16)

        for peer in plane:
            pltpu.make_async_remote_copy(
                src_ref=whole.at[me], dst_ref=whole.at[me], send_sem=ag_send, recv_sem=ag_recv.at[own_group],
                device_id=peer, device_id_type=MESH,
            ).start()

    block_of = div(column_rows((TILE, LANES)), RANK)
    result_ref[...] = jnp.zeros_like(result_ref)

    def contract(steps):
        bases, left = [], []
        for step in steps:
            group = group_at(step)
            bases.append(group * GROUP)

            @pl.when(group == own_group)
            def _():
                wait_bytes(whole, GROUP - 1, ag_recv.at[group])

            @pl.when(group != own_group)
            def _():
                wait_bytes(whole, GROUP, ag_recv.at[group])

        for base in bases:
            for i in range(GROUP):
                tile = whole[base + i].astype(jnp.float32)
                left += [jnp.where(block_of == b, tile, 0.0).astype(jnp.bfloat16) for b in range(BLOCKS)]
        result_ref[...] += jnp.dot(
            jnp.concatenate(left, axis=1), side_by_side(bases), preferred_element_type=jnp.float32
        )

    def contract_pair(step, carry):
        pair = groups // 2 - step
        contract((2 * pair, 2 * pair + 1))
        return carry

    contract((groups - 1,))
    lax.fori_loop(1, groups // 2 + 1, contract_pair, 0)
    result = result_ref[...]

    half = result[:, :LANES] + result[:, LANES:]
    half = half[: 2 * RANK] + half[2 * RANK :]
    terms[dp] = half + pltpu.roll(half, RANK, 0)
    replicas = beside + [device(y, x, core, z_other)] + [device(y, xs[step], core, z) for step in (2, 1, 3)]
    for peer in replicas:
        pltpu.make_async_remote_copy(
            src_ref=terms.at[dp], dst_ref=terms.at[dp], send_sem=dp_send, recv_sem=dp_recv,
            device_id=peer, device_id_type=MESH,
        ).start()

    tiles = jnp.concatenate([whole[chunk] for chunk in range(chunks)], axis=1)
    gram = lax.dot_general(tiles, tiles, (((1,), (1,)), ((), ())), preferred_element_type=jnp.float32)
    lower, inverse = inverse_factor(gram)

    def turn(step, carry):
        for i in range(GROUP):
            chunk = step * GROUP + i
            tile = whole[chunk].astype(jnp.float32)
            twice = jnp.concatenate([tile, tile], axis=0)
            left_ref[chunk] = twice.T.astype(jnp.bfloat16)
        return carry

    lax.fori_loop(0, groups, turn, 0)

    wait_bytes(terms, REPLICAS - 1, dp_recv)
    total = terms[0]
    for i in range(1, REPLICAS):
        total = total + terms[i]
    total = total * (1.0 / REPLICAS)
    columns = []
    for j in range(RANK):
        value = total[j : j + 1, :]
        for k in range(j):
            value = value - lower[j, k] * columns[k]
        columns.append(value * inverse[j])
    weights = [None] * RANK
    for j in reversed(range(RANK)):
        value = columns[j]
        for k in range(j + 1, RANK):
            value = value - lower[k, j] * weights[k]
        weights[j] = value * inverse[j]
    for j in range(RANK):
        factor_ref[j : j + 1, :] = columns[j]
    kind = rem(column_rows((TILE, LANES)), RANK)
    spread = jnp.broadcast_to(weights[0], (TILE, LANES))
    for j in range(1, RANK):
        spread = jnp.where(kind == j, weights[j], spread)
    high = spread.astype(jnp.bfloat16).astype(jnp.float32)
    low = spread - high
    for b in range(BLOCKS):
        at = slice(b * LANES, (b + 1) * LANES)
        pair = [jnp.where(block_of == b, part, 0.0) for part in (high, low)]
        right_ref[:, at] = jnp.concatenate(pair, axis=0).astype(jnp.bfloat16)

    @pl.when(owner)
    def _():
        wait_bytes(outgoing, chunks - 1, rs_send)
        wait_bytes(deep, DEPTH - 1, z_send)
        wait_bytes(arrived, PLANE - 1, ag_send)

    @pl.when(jnp.logical_not(owner))
    def _():
        wait_bytes(outgoing, chunks, rs_send)

    wait_bytes(terms, REPLICAS - 1, dp_send)


def residual_kernel(chunks, m_ref, left_ref, right_ref, factor_ref, out_hbm, factor_hbm, out, sem, factor_sem):
    groups = chunks // GROUP
    factor_copy = pltpu.make_async_copy(factor_ref, factor_hbm, factor_sem)
    factor_copy.start()

    def stores(step):
        at = pl.ds(step * GROUP, GROUP)
        return pltpu.make_async_copy(out.at[at], out_hbm.at[at], sem)

    def work(big, carry):
        for small in range(UNROLL):
            one(big * UNROLL + small)
        return carry

    def one(step):
        for i in range(GROUP):
            chunk = step * GROUP + i
            product = jnp.dot(left_ref[chunk], right_ref[...], preferred_element_type=jnp.float32)
            for b in range(BLOCKS):
                at = slice(b * LANES, (b + 1) * LANES)
                out[chunk, at] = (m_ref[chunk, at] - product[:, at]).astype(jnp.bfloat16)
        stores(step).start()

    lax.fori_loop(0, groups // UNROLL, work, 0)

    pltpu.make_async_copy(out, out_hbm, sem).wait()
    factor_copy.wait()


def per_device(gradient_part, carried_error, query_basis):
    width = gradient_part.shape[3]
    chunks = gradient_part.shape[1] * gradient_part.shape[2] // CHUNK
    tiled = (chunks, CHUNK, width)
    bf16, f32 = jnp.bfloat16, jnp.float32
    hbm = pl.BlockSpec(memory_space=pltpu.HBM)
    vmem = pl.BlockSpec(memory_space=pltpu.VMEM)
    dma = pltpu.SemaphoreType.DMA
    operands = gradient_part.reshape(tiled), carried_error.reshape(tiled), query_basis.T
    operands = [pltpu.with_memory_space_constraint(operand, pltpu.HBM) for operand in operands]
    merged, left, right, factor = pl.pallas_call(
        functools.partial(factor_kernel, chunks),
        out_shape=(
            pltpu.VMEM(tiled, f32),
            pltpu.VMEM((chunks, LANES, 2 * TILE), bf16),
            pltpu.VMEM((2 * TILE, CHUNK), bf16),
            pltpu.VMEM((RANK, width), f32),
        ),
        in_specs=[hbm, hbm, hbm],
        out_specs=(vmem, vmem, vmem, vmem),
        scratch_shapes=[
            pltpu.VMEM((2, *tiled), bf16),
            pltpu.VMEM((RANK, width), f32),
            pltpu.VMEM((chunks, TILE, LANES), bf16),
            pltpu.VMEM((PLANE, TILE, LANES), bf16),
            pltpu.VMEM((DEPTH, TILE, LANES), bf16),
            pltpu.VMEM((chunks, TILE, LANES), bf16),
            pltpu.VMEM((REPLICAS, 2 * RANK, LANES), f32),
            pltpu.VMEM((TILE, 2 * LANES), f32),
            dma((pl.cdiv(chunks // GROUP, 2),)),
            dma, dma, dma, dma, dma, dma,
            dma((chunks // GROUP,)),
            dma, dma,
        ],
        compiler_params=pltpu.CompilerParams(
            collective_id=0, has_side_effects=True, vmem_limit_bytes=24 << 20
        ),
        name="factor",
    )(*operands)
    returned, factor = pl.pallas_call(
        functools.partial(residual_kernel, chunks),
        out_shape=(pltpu.HBM(tiled, bf16), pltpu.HBM((RANK, width), f32)),
        in_specs=[vmem, vmem, vmem, vmem],
        out_specs=(hbm, hbm),
        scratch_shapes=[pltpu.VMEM(tiled, bf16), dma, dma],
        compiler_params=pltpu.CompilerParams(vmem_limit_bytes=16 << 20),
        name="residual",
    )(merged, left, right, factor)
    return returned.reshape(gradient_part.shape), factor.T


def solution(mesh):
    in_specs = (P("dp", None, None, "head"), P("dp", None, None, "head"), P("head", None))
    out_specs = (P("dp", None, None, "head"), P("head", None))
    return jax.shard_map(
        per_device, mesh=mesh, in_specs=in_specs, out_specs=out_specs, check_vma=False
    )
```

```python
import functools
import itertools

import jax
import jax.numpy as jnp
from jax import lax
from jax.experimental import pallas as pl
from jax.experimental.pallas import tpu as pltpu
from jax.sharding import PartitionSpec as P

MESH = pl.DeviceIdType.MESH
RANK = 4
LANES = 128
BLOCKS = 4
CHUNK = BLOCKS * LANES
TILE = BLOCKS * RANK
GROUP = 3
PLANE = 32
DEPTH = 8
REPLICAS = 8
AHEAD = 2
UNROLL = 3
EARLY = 6


def wrap(a, b):
    return jnp.where(a >= b, a - b, a)


def rem(a, b):
    return lax.rem(a, jnp.int32(b))


def div(a, b):
    return lax.div(a, jnp.int32(b))


def place():
    head, dp = lax.axis_index("head"), lax.axis_index("dp")
    core, z_hi, y = rem(head, 2), rem(div(head, 2), 4), div(head, 8)
    x, z_lo = rem(dp, 4), div(dp, 4)
    return y, x, core, z_hi * 2 + z_lo


def device(y, x, core, z):
    return {"head": (y * 4 + div(z, 2)) * 2 + core, "dp": rem(z, 2) * 4 + x}


def of_plane(index, z):
    return device(div(index, 8), rem(div(index, 2), 4), rem(index, 2), z)


def column_rows(shape):
    return lax.broadcasted_iota(jnp.int32, shape, 0)


def inverse_factor(gram):
    rows, columns = column_rows(gram.shape), lax.broadcasted_iota(jnp.int32, gram.shape, 1)

    def entry(j, k):
        picked = (rows - columns == j - k) & ((rows & 3) == j) & ((columns & 3) == k)
        return jnp.sum(jnp.where(picked, gram, 0.0), axis=(0, 1), keepdims=True)

    lower, inverse = {}, []
    for j in range(RANK):
        for k in range(j):
            total = entry(j, k)
            for i in range(k):
                total = total - lower[j, i] * lower[k, i]
            lower[j, k] = total * inverse[k]
        total = entry(j, j)
        for i in range(j):
            total = total - lower[j, i] * lower[j, i]
        inverse.append(1.0 / jnp.sqrt(total))
    return lower, inverse


def factor_kernel(
    chunks, g_hbm, e_hbm, q_hbm, m_ref, left_ref, right_ref, factor_ref,
    ge, rounded, q_ref, outgoing, arrived, deep, whole, terms, result_ref,
    load_sem, q_sem, rs_send, rs_recv, z_send, z_recv, ag_send, ag_recv, dp_send, dp_recv,
):
    y, x, core, z = place()
    me = (y * 4 + x) * 2 + core
    dp = rem(z, 2) * 4 + x
    owner = me < chunks
    groups = chunks // GROUP
    own_group = div(me, GROUP)
    centre = wrap(wrap(own_group, groups), groups)

    def group_at(step):
        reach = groups // 2 - div(jnp.int32(step), 2)
        group = centre + reach * (1 - 2 * rem(jnp.int32(step), 2))
        return wrap(jnp.where(group < 0, group + groups, group), groups)

    def loads(step):
        at = pl.ds(group_at(step) * GROUP, GROUP)
        return [
            pltpu.make_async_copy(src.at[at], ge.at[i, at], load_sem.at[max(step // 2, step - EARLY // 2)])
            for i, src in enumerate((g_hbm, e_hbm))
        ]

    q_copy = pltpu.make_async_copy(q_hbm, q_ref, q_sem)
    q_copy.start()
    for step in range(AHEAD):
        for copy in loads(step):
            copy.start()

    ys = [y] + [wrap(y + step, 4) for step in range(1, 4)]
    xs = [x] + [wrap(x + step, 4) for step in range(1, 4)]
    cores = [core, 1 - core]
    zs = [z] + [wrap(z + step, DEPTH) for step in range(1, DEPTH)]
    z_other = div(z, 2) * 2 + 1 - rem(z, 2)
    far_first = lambda steps, sizes: -sum(min(step, size - step) for step, size in zip(steps, sizes))
    plane = sorted(itertools.product(range(4), range(4), range(2)), key=lambda s: far_first(s, (4, 4, 2)))[:-1]
    line = sorted(range(1, DEPTH), key=lambda s: far_first((s,), (DEPTH,)))
    plane = [device(ys[i], xs[j], cores[k], z) for i, j, k in plane]
    line = [device(y, x, core, zs[step]) for step in line]
    beside = [device(y, xs[step], core, z_other) for step in (2, 1, 3)]

    barrier = pltpu.get_barrier_semaphore()
    greeted = plane + line + beside
    for peer in greeted:
        pl.semaphore_signal(barrier, inc=1, device_id=peer, device_id_type=MESH)

    q_copy.wait()
    for step in range(AHEAD, groups):
        for copy in loads(step):
            copy.start()
    q = q_ref[...]
    high = q.astype(jnp.bfloat16).astype(jnp.float32)
    both = jnp.concatenate([high, q - high], axis=0)
    q_rows = both.astype(jnp.bfloat16)
    upper = column_rows((2 * RANK, LANES)) < RANK

    def rows_of(bases):
        return jnp.concatenate(
            [rounded[pl.ds(base, GROUP)].reshape(GROUP * CHUNK, LANES) for base in bases], axis=0
        )

    def project(first, count, sem):
        bases = [group_at(first + i) * GROUP for i in range(count)]
        done = ge.at[:, pl.ds(0, count * GROUP)]
        pltpu.make_async_copy(done, done, load_sem.at[sem]).wait()
        for base in bases:
            at = pl.ds(base, GROUP)
            rounded[at] = ge[0, at] + ge[1, at]
        product = lax.dot_general(
            q_rows, rows_of(bases), (((1,), (1,)), ((), ())), preferred_element_type=jnp.float32
        )
        total = product + pltpu.roll(product, RANK, 0)
        for i in range(count * GROUP):
            starts = [i * CHUNK + b * LANES for b in range(BLOCKS)]
            pieces = [total[:, start : start + LANES] for start in starts]
            tile = jnp.concatenate(
                [jnp.where(upper, pieces[0], pieces[1]), jnp.where(upper, pieces[2], pieces[3])], axis=0
            )
            outgoing[bases[i // GROUP] + i % GROUP] = tile.astype(jnp.bfloat16)

    def project_pair(pair, carry):
        project(2 * pair, 2, pair)
        return carry

    lax.fori_loop(0, EARLY // 2, project_pair, 0)

    pl.semaphore_wait(barrier, len(greeted))

    def send_terms(step, carry):
        for i in range(GROUP):
            chunk = group_at(step) * GROUP + i

            @pl.when(chunk != me)
            def _():
                pltpu.make_async_remote_copy(
                    src_ref=outgoing.at[chunk], dst_ref=arrived.at[me], send_sem=rs_send, recv_sem=rs_recv,
                    device_id=of_plane(chunk, z), device_id_type=MESH,
                ).start()

        return carry

    lax.fori_loop(0, EARLY, send_terms, 0)
    for step in range(EARLY, groups):
        project(step, 1, step - EARLY // 2)
        send_terms(step, 0)

    @pl.when(owner)
    def _():
        arrived[me] = outgoing[me]

    def merge(chunk, carry):
        m_ref[chunk] = ge[0, chunk].astype(jnp.float32) + ge[1, chunk].astype(jnp.float32)
        return carry

    lax.fori_loop(0, chunks, merge, 0)

    def wait_bytes(ref, count, sem):
        at = ref.at[pl.ds(0, count)]
        pltpu.make_async_copy(at, at, sem).wait()

    @pl.when(owner)
    def _():
        wait_bytes(arrived, PLANE - 1, rs_recv)
        total = arrived[0].astype(jnp.float32)
        for i in range(1, PLANE):
            total = total + arrived[i].astype(jnp.float32)
        deep[z] = total.astype(jnp.bfloat16)
        for peer in line:
            pltpu.make_async_remote_copy(
                src_ref=deep.at[z], dst_ref=deep.at[z], send_sem=z_send, recv_sem=z_recv,
                device_id=peer, device_id_type=MESH,
            ).start()
        wait_bytes(deep, DEPTH - 1, z_recv)
        total = deep[0].astype(jnp.float32)
        for i in range(1, DEPTH):
            total = total + deep[i].astype(jnp.float32)
        whole[me] = total.astype(jnp.bfloat16)

        for peer in plane:
            pltpu.make_async_remote_copy(
                src_ref=whole.at[me], dst_ref=whole.at[me], send_sem=ag_send, recv_sem=ag_recv.at[own_group],
                device_id=peer, device_id_type=MESH,
            ).start()

    block_of = div(column_rows((TILE, LANES)), RANK)
    result_ref[...] = jnp.zeros_like(result_ref)

    def contract(steps):
        bases, left = [], []
        for step in steps:
            group = group_at(step)
            bases.append(group * GROUP)

            @pl.when(group == own_group)
            def _():
                wait_bytes(whole, GROUP - 1, ag_recv.at[group])

            @pl.when(group != own_group)
            def _():
                wait_bytes(whole, GROUP, ag_recv.at[group])

        for base in bases:
            for i in range(GROUP):
                tile = whole[base + i].astype(jnp.float32)
                left += [jnp.where(block_of == b, tile, 0.0).astype(jnp.bfloat16) for b in range(BLOCKS)]
        result_ref[...] += jnp.dot(
            jnp.concatenate(left, axis=1), rows_of(bases), preferred_element_type=jnp.float32
        )

    def contract_pair(step, carry):
        pair = groups // 2 - step
        contract((2 * pair, 2 * pair + 1))
        return carry

    contract((groups - 1,))
    lax.fori_loop(1, groups // 2 + 1, contract_pair, 0)
    result = result_ref[...]

    half = result[: 2 * RANK] + result[2 * RANK :]
    terms[dp] = half + pltpu.roll(half, RANK, 0)
    replicas = beside + [device(y, x, core, z_other)] + [device(y, xs[step], core, z) for step in (2, 1, 3)]
    for peer in replicas:
        pltpu.make_async_remote_copy(
            src_ref=terms.at[dp], dst_ref=terms.at[dp], send_sem=dp_send, recv_sem=dp_recv,
            device_id=peer, device_id_type=MESH,
        ).start()

    tiles = jnp.concatenate([whole[chunk] for chunk in range(chunks)], axis=1)
    gram = lax.dot_general(tiles, tiles, (((1,), (1,)), ((), ())), preferred_element_type=jnp.float32)
    lower, inverse = inverse_factor(gram)

    def turn(step, carry):
        for i in range(GROUP):
            chunk = step * GROUP + i
            tile = whole[chunk].astype(jnp.float32)
            twice = jnp.concatenate([tile, tile], axis=0)
            left_ref[chunk] = twice.T.astype(jnp.bfloat16)
        return carry

    lax.fori_loop(0, groups, turn, 0)

    wait_bytes(terms, REPLICAS - 1, dp_recv)
    total = terms[0]
    for i in range(1, REPLICAS):
        total = total + terms[i]
    total = total * (1.0 / REPLICAS)
    columns = []
    for j in range(RANK):
        value = total[j : j + 1, :]
        for k in range(j):
            value = value - lower[j, k] * columns[k]
        columns.append(value * inverse[j])
    weights = [None] * RANK
    for j in reversed(range(RANK)):
        value = columns[j]
        for k in range(j + 1, RANK):
            value = value - lower[k, j] * weights[k]
        weights[j] = value * inverse[j]
    for j in range(RANK):
        factor_ref[j : j + 1, :] = columns[j]
    kind = rem(column_rows((TILE, LANES)), RANK)
    spread = jnp.broadcast_to(weights[0], (TILE, LANES))
    for j in range(1, RANK):
        spread = jnp.where(kind == j, weights[j], spread)
    high = spread.astype(jnp.bfloat16).astype(jnp.float32)
    low = spread - high
    for b in range(BLOCKS):
        at = slice(b * LANES, (b + 1) * LANES)
        pair = [jnp.where(block_of == b, part, 0.0) for part in (high, low)]
        right_ref[:, at] = jnp.concatenate(pair, axis=0).astype(jnp.bfloat16)

    @pl.when(owner)
    def _():
        wait_bytes(outgoing, chunks - 1, rs_send)
        wait_bytes(deep, DEPTH - 1, z_send)
        wait_bytes(arrived, PLANE - 1, ag_send)

    @pl.when(jnp.logical_not(owner))
    def _():
        wait_bytes(outgoing, chunks, rs_send)

    wait_bytes(terms, REPLICAS - 1, dp_send)


def residual_kernel(chunks, m_ref, left_ref, right_ref, factor_ref, out_hbm, factor_hbm, out, sem, factor_sem):
    groups = chunks // GROUP
    factor_copy = pltpu.make_async_copy(factor_ref, factor_hbm, factor_sem)
    factor_copy.start()

    def stores(step):
        at = pl.ds(step * GROUP, GROUP)
        return pltpu.make_async_copy(out.at[at], out_hbm.at[at], sem)

    def work(big, carry):
        for small in range(UNROLL):
            one(big * UNROLL + small)
        return carry

    def one(step):
        for i in range(GROUP):
            chunk = step * GROUP + i
            product = jnp.dot(left_ref[chunk], right_ref[...], preferred_element_type=jnp.float32)
            for b in range(BLOCKS):
                at = slice(b * LANES, (b + 1) * LANES)
                out[chunk, at] = (m_ref[chunk, at] - product[:, at]).astype(jnp.bfloat16)
        stores(step).start()

    lax.fori_loop(0, groups // UNROLL, work, 0)

    pltpu.make_async_copy(out, out_hbm, sem).wait()
    factor_copy.wait()


def per_device(gradient_part, carried_error, query_basis):
    width = gradient_part.shape[3]
    chunks = gradient_part.shape[1] * gradient_part.shape[2] // CHUNK
    tiled = (chunks, CHUNK, width)
    bf16, f32 = jnp.bfloat16, jnp.float32
    hbm = pl.BlockSpec(memory_space=pltpu.HBM)
    vmem = pl.BlockSpec(memory_space=pltpu.VMEM)
    dma = pltpu.SemaphoreType.DMA
    operands = gradient_part.reshape(tiled), carried_error.reshape(tiled), query_basis.T
    operands = [pltpu.with_memory_space_constraint(operand, pltpu.HBM) for operand in operands]
    merged, left, right, factor = pl.pallas_call(
        functools.partial(factor_kernel, chunks),
        out_shape=(
            pltpu.VMEM(tiled, f32),
            pltpu.VMEM((chunks, LANES, 2 * TILE), bf16),
            pltpu.VMEM((2 * TILE, CHUNK), bf16),
            pltpu.VMEM((RANK, width), f32),
        ),
        in_specs=[hbm, hbm, hbm],
        out_specs=(vmem, vmem, vmem, vmem),
        scratch_shapes=[
            pltpu.VMEM((2, *tiled), bf16),
            pltpu.VMEM(tiled, bf16),
            pltpu.VMEM((RANK, width), f32),
            pltpu.VMEM((chunks, TILE, LANES), bf16),
            pltpu.VMEM((PLANE, TILE, LANES), bf16),
            pltpu.VMEM((DEPTH, TILE, LANES), bf16),
            pltpu.VMEM((chunks, TILE, LANES), bf16),
            pltpu.VMEM((REPLICAS, 2 * RANK, LANES), f32),
            pltpu.VMEM((TILE, LANES), f32),
            dma((chunks // GROUP - EARLY // 2,)),
            dma, dma, dma, dma, dma, dma,
            dma((chunks // GROUP,)),
            dma, dma,
        ],
        compiler_params=pltpu.CompilerParams(
            collective_id=0, has_side_effects=True, vmem_limit_bytes=28 << 20
        ),
        name="factor",
    )(*operands)
    returned, factor = pl.pallas_call(
        functools.partial(residual_kernel, chunks),
        out_shape=(pltpu.HBM(tiled, bf16), pltpu.HBM((RANK, width), f32)),
        in_specs=[vmem, vmem, vmem, vmem],
        out_specs=(hbm, hbm),
        scratch_shapes=[pltpu.VMEM(tiled, bf16), dma, dma],
        compiler_params=pltpu.CompilerParams(vmem_limit_bytes=16 << 20),
        name="residual",
    )(merged, left, right, factor)
    return returned.reshape(gradient_part.shape), factor.T


def solution(mesh):
    in_specs = (P("dp", None, None, "head"), P("dp", None, None, "head"), P("head", None))
    out_specs = (P("dp", None, None, "head"), P("head", None))
    return jax.shard_map(
        per_device, mesh=mesh, in_specs=in_specs, out_specs=out_specs, check_vma=False
    )
```

```python
import functools
import itertools

import jax
import jax.numpy as jnp
from jax import lax
from jax.experimental import pallas as pl
from jax.experimental.pallas import tpu as pltpu
from jax.sharding import PartitionSpec as P

MESH = pl.DeviceIdType.MESH
RANK = 4
LANES = 128
BLOCKS = 4
CHUNK = BLOCKS * LANES
TILE = BLOCKS * RANK
GROUP = 3
PLANE = 32
DEPTH = 8
REPLICAS = 8
AHEAD = 2
EARLY = 6


def wrap(a, b):
    return jnp.where(a >= b, a - b, a)


def rem(a, b):
    return lax.rem(a, jnp.int32(b))


def div(a, b):
    return lax.div(a, jnp.int32(b))


def place():
    head, dp = lax.axis_index("head"), lax.axis_index("dp")
    core, z_hi, y = rem(head, 2), rem(div(head, 2), 4), div(head, 8)
    x, z_lo = rem(dp, 4), div(dp, 4)
    return y, x, core, z_hi * 2 + z_lo


def device(y, x, core, z):
    return {"head": (y * 4 + div(z, 2)) * 2 + core, "dp": rem(z, 2) * 4 + x}


def turned(row, column):
    return column + rem(row, 2) * (3 - 2 * column)


def number_of(y, x, core):
    row = wrap(y + 3, 4)
    return (row * 4 + turned(row, x)) * 2 + core


def of_plane(index, z):
    row = div(index, 8)
    return device(wrap(row + 1, 4), turned(row, rem(div(index, 2), 4)), rem(index, 2), z)


def column_rows(shape):
    return lax.broadcasted_iota(jnp.int32, shape, 0)


def inverse_factor(gram):
    rows, columns = column_rows(gram.shape), lax.broadcasted_iota(jnp.int32, gram.shape, 1)

    def entry(j, k):
        picked = (rows - columns == j - k) & ((rows & 3) == j) & ((columns & 3) == k)
        return jnp.sum(jnp.where(picked, gram, 0.0), axis=(0, 1), keepdims=True)

    lower, inverse = {}, []
    for j in range(RANK):
        for k in range(j):
            total = entry(j, k)
            for i in range(k):
                total = total - lower[j, i] * lower[k, i]
            lower[j, k] = total * inverse[k]
        total = entry(j, j)
        for i in range(j):
            total = total - lower[j, i] * lower[j, i]
        inverse.append(1.0 / jnp.sqrt(total))
    return lower, inverse


def factor_kernel(
    chunks, g_hbm, e_hbm, q_hbm, m_ref, left_ref, right_ref, factor_ref,
    ge, rounded, q_ref, outgoing, arrived, deep, whole, terms, result_ref,
    load_sem, q_sem, rs_send, rs_recv, z_send, z_recv, ag_send, ag_recv, dp_send, dp_recv,
):
    y, x, core, z = place()
    me = number_of(y, x, core)
    dp = rem(z, 2) * 4 + x
    owner = me < chunks
    groups = chunks // GROUP
    own_group = div(me, GROUP)
    centre = wrap(wrap(own_group, groups), groups)

    def group_at(step):
        reach = groups // 2 - div(jnp.int32(step), 2)
        group = centre + reach * (1 - 2 * rem(jnp.int32(step), 2))
        return wrap(jnp.where(group < 0, group + groups, group), groups)

    def loads(step):
        at = pl.ds(group_at(step) * GROUP, GROUP)
        return [
            pltpu.make_async_copy(src.at[at], ge.at[i, at], load_sem.at[max(step // 2, step - EARLY // 2)])
            for i, src in enumerate((g_hbm, e_hbm))
        ]

    q_copy = pltpu.make_async_copy(q_hbm, q_ref, q_sem)
    q_copy.start()
    for step in range(AHEAD):
        for copy in loads(step):
            copy.start()

    ys = [y] + [wrap(y + step, 4) for step in range(1, 4)]
    xs = [x] + [wrap(x + step, 4) for step in range(1, 4)]
    cores = [core, 1 - core]
    zs = [z] + [wrap(z + step, DEPTH) for step in range(1, DEPTH)]
    z_other = div(z, 2) * 2 + 1 - rem(z, 2)
    far_first = lambda steps, sizes: -sum(min(step, size - step) for step, size in zip(steps, sizes))
    plane = sorted(itertools.product(range(4), range(4), range(2)), key=lambda s: far_first(s, (4, 4, 2)))[:-1]
    line = sorted(range(1, DEPTH), key=lambda s: far_first((s,), (DEPTH,)))
    plane = [device(ys[i], xs[j], cores[k], z) for i, j, k in plane]
    line = [device(y, x, core, zs[step]) for step in line]
    beside = [device(y, xs[step], core, z_other) for step in (2, 1, 3)]

    barrier = pltpu.get_barrier_semaphore()
    greeted = plane + line + beside
    for peer in greeted:
        pl.semaphore_signal(barrier, inc=1, device_id=peer, device_id_type=MESH)

    q_copy.wait()
    for step in range(AHEAD, groups):
        for copy in loads(step):
            copy.start()
    q = q_ref[...]
    high = q.astype(jnp.bfloat16).astype(jnp.float32)
    both = jnp.concatenate([high, q - high], axis=0)
    q_rows = both.astype(jnp.bfloat16)
    upper = column_rows((2 * RANK, LANES)) < RANK

    def rows_of(bases):
        return jnp.concatenate(
            [rounded[pl.ds(base, GROUP)].reshape(GROUP * CHUNK, LANES) for base in bases], axis=0
        )

    def project(first, count, sem):
        bases = [group_at(first + i) * GROUP for i in range(count)]
        done = ge.at[:, pl.ds(0, count * GROUP)]
        pltpu.make_async_copy(done, done, load_sem.at[sem]).wait()
        for base in bases:
            at = pl.ds(base, GROUP)
            rounded[at] = ge[0, at] + ge[1, at]
        product = lax.dot_general(
            q_rows, rows_of(bases), (((1,), (1,)), ((), ())), preferred_element_type=jnp.float32
        )
        total = product + pltpu.roll(product, RANK, 0)
        for i in range(count * GROUP):
            starts = [i * CHUNK + b * LANES for b in range(BLOCKS)]
            pieces = [total[:, start : start + LANES] for start in starts]
            tile = jnp.concatenate(
                [jnp.where(upper, pieces[0], pieces[1]), jnp.where(upper, pieces[2], pieces[3])], axis=0
            )
            outgoing[bases[i // GROUP] + i % GROUP] = tile.astype(jnp.bfloat16)

    def project_pair(pair, carry):
        project(2 * pair, 2, pair)
        return carry

    lax.fori_loop(0, EARLY // 2, project_pair, 0)

    pl.semaphore_wait(barrier, len(greeted))

    def send_terms(step, carry):
        for i in range(GROUP):
            chunk = group_at(step) * GROUP + i

            @pl.when(chunk != me)
            def _():
                pltpu.make_async_remote_copy(
                    src_ref=outgoing.at[chunk], dst_ref=arrived.at[me], send_sem=rs_send, recv_sem=rs_recv,
                    device_id=of_plane(chunk, z), device_id_type=MESH,
                ).start()

        return carry

    lax.fori_loop(0, EARLY, send_terms, 0)
    for step in range(EARLY, groups):
        project(step, 1, step - EARLY // 2)
        send_terms(step, 0)

    @pl.when(owner)
    def _():
        arrived[me] = outgoing[me]

    def merge(chunk, carry):
        m_ref[chunk] = ge[0, chunk].astype(jnp.float32) + ge[1, chunk].astype(jnp.float32)
        return carry

    lax.fori_loop(0, chunks, merge, 0)

    def wait_bytes(ref, count, sem):
        at = ref.at[pl.ds(0, count)]
        pltpu.make_async_copy(at, at, sem).wait()

    @pl.when(owner)
    def _():
        wait_bytes(arrived, PLANE - 1, rs_recv)
        total = arrived[0].astype(jnp.float32)
        for i in range(1, PLANE):
            total = total + arrived[i].astype(jnp.float32)
        deep[z] = total.astype(jnp.bfloat16)
        for peer in line:
            pltpu.make_async_remote_copy(
                src_ref=deep.at[z], dst_ref=deep.at[z], send_sem=z_send, recv_sem=z_recv,
                device_id=peer, device_id_type=MESH,
            ).start()
        wait_bytes(deep, DEPTH - 1, z_recv)
        total = deep[0].astype(jnp.float32)
        for i in range(1, DEPTH):
            total = total + deep[i].astype(jnp.float32)
        whole[me] = total.astype(jnp.bfloat16)

        for peer in plane:
            pltpu.make_async_remote_copy(
                src_ref=whole.at[me], dst_ref=whole.at[me], send_sem=ag_send, recv_sem=ag_recv.at[own_group],
                device_id=peer, device_id_type=MESH,
            ).start()

    block_of = div(column_rows((TILE, LANES)), RANK)
    result_ref[...] = jnp.zeros_like(result_ref)

    def contract(steps):
        bases, left = [], []
        for step in steps:
            group = group_at(step)
            bases.append(group * GROUP)

            @pl.when(group == own_group)
            def _():
                wait_bytes(whole, GROUP - 1, ag_recv.at[group])

            @pl.when(group != own_group)
            def _():
                wait_bytes(whole, GROUP, ag_recv.at[group])

        for base in bases:
            for i in range(GROUP):
                tile = whole[base + i].astype(jnp.float32)
                left += [jnp.where(block_of == b, tile, 0.0).astype(jnp.bfloat16) for b in range(BLOCKS)]
        result_ref[...] += jnp.dot(
            jnp.concatenate(left, axis=1), rows_of(bases), preferred_element_type=jnp.float32
        )

    def contract_pair(step, carry):
        pair = groups // 2 - step
        contract((2 * pair, 2 * pair + 1))
        return carry

    contract((groups - 1,))
    lax.fori_loop(1, groups // 2 + 1, contract_pair, 0)
    result = result_ref[...]

    half = result[: 2 * RANK] + result[2 * RANK :]
    terms[dp] = half + pltpu.roll(half, RANK, 0)
    replicas = beside + [device(y, x, core, z_other)] + [device(y, xs[step], core, z) for step in (2, 1, 3)]
    for peer in replicas:
        pltpu.make_async_remote_copy(
            src_ref=terms.at[dp], dst_ref=terms.at[dp], send_sem=dp_send, recv_sem=dp_recv,
            device_id=peer, device_id_type=MESH,
        ).start()

    tiles = jnp.concatenate([whole[chunk] for chunk in range(chunks)], axis=1)
    gram = lax.dot_general(tiles, tiles, (((1,), (1,)), ((), ())), preferred_element_type=jnp.float32)
    lower, inverse = inverse_factor(gram)

    def turn(step, carry):
        for i in range(GROUP):
            chunk = step * GROUP + i
            tile = whole[chunk].astype(jnp.float32)
            twice = jnp.concatenate([tile, tile], axis=0)
            left_ref[chunk] = twice.T.astype(jnp.bfloat16)
        return carry

    lax.fori_loop(0, groups, turn, 0)

    wait_bytes(terms, REPLICAS - 1, dp_recv)
    total = terms[0]
    for i in range(1, REPLICAS):
        total = total + terms[i]
    total = total * (1.0 / REPLICAS)
    columns = []
    for j in range(RANK):
        value = total[j : j + 1, :]
        for k in range(j):
            value = value - lower[j, k] * columns[k]
        columns.append(value * inverse[j])
    weights = [None] * RANK
    for j in reversed(range(RANK)):
        value = columns[j]
        for k in range(j + 1, RANK):
            value = value - lower[k, j] * weights[k]
        weights[j] = value * inverse[j]
    for j in range(RANK):
        factor_ref[j : j + 1, :] = columns[j]
    kind = rem(column_rows((TILE, LANES)), RANK)
    spread = jnp.broadcast_to(weights[0], (TILE, LANES))
    for j in range(1, RANK):
        spread = jnp.where(kind == j, weights[j], spread)
    high = spread.astype(jnp.bfloat16).astype(jnp.float32)
    low = spread - high
    for b in range(BLOCKS):
        at = slice(b * LANES, (b + 1) * LANES)
        pair = [jnp.where(block_of == b, part, 0.0) for part in (high, low)]
        right_ref[:, at] = jnp.concatenate(pair, axis=0).astype(jnp.bfloat16)

    @pl.when(owner)
    def _():
        wait_bytes(outgoing, chunks - 1, rs_send)
        wait_bytes(deep, DEPTH - 1, z_send)
        wait_bytes(arrived, PLANE - 1, ag_send)

    @pl.when(jnp.logical_not(owner))
    def _():
        wait_bytes(outgoing, chunks, rs_send)

    wait_bytes(terms, REPLICAS - 1, dp_send)


def residual_kernel(chunks, m_ref, left_ref, right_ref, factor_ref, out_hbm, factor_hbm, out, sem, factor_sem):
    factor_copy = pltpu.make_async_copy(factor_ref, factor_hbm, factor_sem)

    for chunk in range(chunks):
        product = jnp.dot(left_ref[chunk], right_ref[...], preferred_element_type=jnp.float32)
        for b in range(BLOCKS):
            at = slice(b * LANES, (b + 1) * LANES)
            out[chunk, at] = (m_ref[chunk, at] - product[:, at]).astype(jnp.bfloat16)
        pltpu.make_async_copy(out.at[chunk], out_hbm.at[chunk], sem).start()
    factor_copy.start()
    pltpu.make_async_copy(out, out_hbm, sem).wait()
    factor_copy.wait()


def per_device(gradient_part, carried_error, query_basis):
    width = gradient_part.shape[3]
    chunks = gradient_part.shape[1] * gradient_part.shape[2] // CHUNK
    tiled = (chunks, CHUNK, width)
    bf16, f32 = jnp.bfloat16, jnp.float32
    hbm = pl.BlockSpec(memory_space=pltpu.HBM)
    vmem = pl.BlockSpec(memory_space=pltpu.VMEM)
    dma = pltpu.SemaphoreType.DMA
    operands = gradient_part.reshape(tiled), carried_error.reshape(tiled), query_basis.T
    operands = [pltpu.with_memory_space_constraint(operand, pltpu.HBM) for operand in operands]
    merged, left, right, factor = pl.pallas_call(
        functools.partial(factor_kernel, chunks),
        out_shape=(
            pltpu.VMEM(tiled, f32),
            pltpu.VMEM((chunks, LANES, 2 * TILE), bf16),
            pltpu.VMEM((2 * TILE, CHUNK), bf16),
            pltpu.VMEM((RANK, width), f32),
        ),
        in_specs=[hbm, hbm, hbm],
        out_specs=(vmem, vmem, vmem, vmem),
        scratch_shapes=[
            pltpu.VMEM((2, *tiled), bf16),
            pltpu.VMEM(tiled, bf16),
            pltpu.VMEM((RANK, width), f32),
            pltpu.VMEM((chunks, TILE, LANES), bf16),
            pltpu.VMEM((PLANE, TILE, LANES), bf16),
            pltpu.VMEM((DEPTH, TILE, LANES), bf16),
            pltpu.VMEM((chunks, TILE, LANES), bf16),
            pltpu.VMEM((REPLICAS, 2 * RANK, LANES), f32),
            pltpu.VMEM((TILE, LANES), f32),
            dma((chunks // GROUP - EARLY // 2,)),
            dma, dma, dma, dma, dma, dma,
            dma((chunks // GROUP,)),
            dma, dma,
        ],
        compiler_params=pltpu.CompilerParams(
            collective_id=0, has_side_effects=True, vmem_limit_bytes=28 << 20
        ),
        name="factor",
    )(*operands)
    returned, factor = pl.pallas_call(
        functools.partial(residual_kernel, chunks),
        out_shape=(pltpu.HBM(tiled, bf16), pltpu.HBM((RANK, width), f32)),
        in_specs=[vmem, vmem, vmem, vmem],
        out_specs=(hbm, hbm),
        scratch_shapes=[pltpu.VMEM(tiled, bf16), dma, dma],
        compiler_params=pltpu.CompilerParams(vmem_limit_bytes=16 << 20),
        name="residual",
    )(merged, left, right, factor)
    return returned.reshape(gradient_part.shape), factor.T


def solution(mesh):
    in_specs = (P("dp", None, None, "head"), P("dp", None, None, "head"), P("head", None))
    out_specs = (P("dp", None, None, "head"), P("head", None))
    return jax.shard_map(
        per_device, mesh=mesh, in_specs=in_specs, out_specs=out_specs, check_vma=False
    )
```

```python
import functools
import itertools

import jax
import jax.numpy as jnp
from jax import lax
from jax.experimental import pallas as pl
from jax.experimental.pallas import tpu as pltpu
from jax.sharding import PartitionSpec as P

MESH = pl.DeviceIdType.MESH
RANK = 4
LANES = 128
BLOCKS = 4
CHUNK = BLOCKS * LANES
TILE = BLOCKS * RANK
GROUP = 3
PLANE = 32
DEPTH = 8
REPLICAS = 8
AHEAD = 2
EARLY = 6


def wrap(a, b):
    return jnp.where(a >= b, a - b, a)


def rem(a, b):
    return lax.rem(a, jnp.int32(b))


def div(a, b):
    return lax.div(a, jnp.int32(b))


def place():
    head, dp = lax.axis_index("head"), lax.axis_index("dp")
    core, z_hi, y = rem(head, 2), rem(div(head, 2), 4), div(head, 8)
    x, z_lo = rem(dp, 4), div(dp, 4)
    return y, x, core, z_hi * 2 + z_lo


def device(y, x, core, z):
    return {"head": (y * 4 + div(z, 2)) * 2 + core, "dp": rem(z, 2) * 4 + x}


def turned(row, column):
    return column + rem(row, 2) * (3 - 2 * column)


def number_of(y, x, core):
    row = wrap(y + 3, 4)
    return (row * 4 + turned(row, x)) * 2 + core


def of_plane(index, z):
    row = div(index, 8)
    return device(wrap(row + 1, 4), turned(row, rem(div(index, 2), 4)), rem(index, 2), z)


def column_rows(shape):
    return lax.broadcasted_iota(jnp.int32, shape, 0)


def inverse_factor(gram):
    rows, columns = column_rows(gram.shape), lax.broadcasted_iota(jnp.int32, gram.shape, 1)

    def entry(j, k):
        picked = (rows - columns == j - k) & ((rows & 3) == j) & ((columns & 3) == k)
        return jnp.sum(jnp.where(picked, gram, 0.0), axis=(0, 1), keepdims=True)

    lower, inverse = {}, []
    for j in range(RANK):
        for k in range(j):
            total = entry(j, k)
            for i in range(k):
                total = total - lower[j, i] * lower[k, i]
            lower[j, k] = total * inverse[k]
        total = entry(j, j)
        for i in range(j):
            total = total - lower[j, i] * lower[j, i]
        inverse.append(1.0 / jnp.sqrt(total))
    return lower, inverse


def factor_kernel(
    chunks, g_hbm, e_hbm, q_hbm, m_ref, left_ref, right_ref, factor_ref,
    ge, rounded, q_ref, outgoing, arrived, deep, whole, terms, result_ref,
    rs_recv, z_recv, ag_recv, dp_recv,
):
    dma = pltpu.SemaphoreType.DMA
    pl.run_scoped(
        functools.partial(
            factor_body, chunks, g_hbm, e_hbm, q_hbm, m_ref, left_ref, right_ref, factor_ref,
            ge, rounded, q_ref, outgoing, arrived, deep, whole, terms, result_ref,
            rs_recv, z_recv, ag_recv, dp_recv,
        ),
        dma((chunks // GROUP - EARLY // 2,)), dma, dma, dma, dma, dma,
    )


def factor_body(
    chunks, g_hbm, e_hbm, q_hbm, m_ref, left_ref, right_ref, factor_ref,
    ge, rounded, q_ref, outgoing, arrived, deep, whole, terms, result_ref,
    rs_recv, z_recv, ag_recv, dp_recv,
    load_sem, q_sem, rs_send, z_send, ag_send, dp_send,
):
    y, x, core, z = place()
    me = number_of(y, x, core)
    dp = rem(z, 2) * 4 + x
    owner = me < chunks
    groups = chunks // GROUP
    own_group = div(me, GROUP)
    centre = wrap(wrap(own_group, groups), groups)

    def group_at(step):
        reach = groups // 2 - div(jnp.int32(step), 2)
        group = centre + reach * (1 - 2 * rem(jnp.int32(step), 2))
        return wrap(jnp.where(group < 0, group + groups, group), groups)

    def loads(step):
        at = pl.ds(group_at(step) * GROUP, GROUP)
        return [
            pltpu.make_async_copy(src.at[at], ge.at[i, at], load_sem.at[max(step // 2, step - EARLY // 2)])
            for i, src in enumerate((g_hbm, e_hbm))
        ]

    q_copy = pltpu.make_async_copy(q_hbm, q_ref, q_sem)
    q_copy.start()
    for step in range(AHEAD):
        for copy in loads(step):
            copy.start()

    ys = [y] + [wrap(y + step, 4) for step in range(1, 4)]
    xs = [x] + [wrap(x + step, 4) for step in range(1, 4)]
    cores = [core, 1 - core]
    zs = [z] + [wrap(z + step, DEPTH) for step in range(1, DEPTH)]
    z_other = div(z, 2) * 2 + 1 - rem(z, 2)
    far_first = lambda steps, sizes: -sum(min(step, size - step) for step, size in zip(steps, sizes))
    plane = sorted(itertools.product(range(4), range(4), range(2)), key=lambda s: far_first(s, (4, 4, 2)))[:-1]
    line = sorted(range(1, DEPTH), key=lambda s: far_first((s,), (DEPTH,)))
    plane = [device(ys[i], xs[j], cores[k], z) for i, j, k in plane]
    line = [device(y, x, core, zs[step]) for step in line]
    beside = [device(y, xs[step], core, z_other) for step in (2, 1, 3)]

    barrier = pltpu.get_barrier_semaphore()
    greeted = plane + line + beside
    for peer in plane:
        pl.semaphore_signal(barrier, inc=1, device_id=peer, device_id_type=MESH)

    q_copy.wait()
    for step in range(AHEAD, groups):
        for copy in loads(step):
            copy.start()
    for peer in line + beside:
        pl.semaphore_signal(barrier, inc=1, device_id=peer, device_id_type=MESH)
    q = q_ref[...]
    high = q.astype(jnp.bfloat16).astype(jnp.float32)
    both = jnp.concatenate([high, q - high], axis=0)
    q_rows = both.astype(jnp.bfloat16)
    upper = column_rows((2 * RANK, LANES)) < RANK

    def rows_of(bases):
        return jnp.concatenate(
            [rounded[pl.ds(base, GROUP)].reshape(GROUP * CHUNK, LANES) for base in bases], axis=0
        )

    def project(first, count, sem):
        bases = [group_at(first + i) * GROUP for i in range(count)]
        done = ge.at[:, pl.ds(0, count * GROUP)]
        pltpu.make_async_copy(done, done, load_sem.at[sem]).wait()
        for base in bases:
            at = pl.ds(base, GROUP)
            rounded[at] = ge[0, at] + ge[1, at]
        product = lax.dot_general(
            q_rows, rows_of(bases), (((1,), (1,)), ((), ())), preferred_element_type=jnp.float32
        )
        total = product + pltpu.roll(product, RANK, 0)
        for i in range(count * GROUP):
            starts = [i * CHUNK + b * LANES for b in range(BLOCKS)]
            pieces = [total[:, start : start + LANES] for start in starts]
            tile = jnp.concatenate(
                [jnp.where(upper, pieces[0], pieces[1]), jnp.where(upper, pieces[2], pieces[3])], axis=0
            )
            outgoing[bases[i // GROUP] + i % GROUP] = tile.astype(jnp.bfloat16)

    def project_pair(pair, carry):
        project(2 * pair, 2, pair)
        return carry

    lax.fori_loop(0, EARLY // 2, project_pair, 0)

    pl.semaphore_wait(barrier, len(greeted))

    def send_terms(step, carry):
        for i in range(GROUP):
            chunk = group_at(step) * GROUP + i

            @pl.when(chunk != me)
            def _():
                pltpu.make_async_remote_copy(
                    src_ref=outgoing.at[chunk], dst_ref=arrived.at[me], send_sem=rs_send, recv_sem=rs_recv,
                    device_id=of_plane(chunk, z), device_id_type=MESH,
                ).start()

        return carry

    lax.fori_loop(0, EARLY, send_terms, 0)
    for step in range(EARLY, groups):
        project(step, 1, step - EARLY // 2)
        send_terms(step, 0)

    @pl.when(owner)
    def _():
        arrived[me] = outgoing[me]

    def merge(chunk, carry):
        m_ref[chunk] = ge[0, chunk].astype(jnp.float32) + ge[1, chunk].astype(jnp.float32)
        return carry

    lax.fori_loop(0, chunks, merge, 0)

    def wait_bytes(ref, count, sem):
        at = ref.at[pl.ds(0, count)]
        pltpu.make_async_copy(at, at, sem).wait()

    @pl.when(owner)
    def _():
        wait_bytes(arrived, PLANE - 1, rs_recv)
        total = arrived[0].astype(jnp.float32)
        for i in range(1, PLANE):
            total = total + arrived[i].astype(jnp.float32)
        deep[z] = total.astype(jnp.bfloat16)
        for peer in line:
            pltpu.make_async_remote_copy(
                src_ref=deep.at[z], dst_ref=deep.at[z], send_sem=z_send, recv_sem=z_recv,
                device_id=peer, device_id_type=MESH,
            ).start()
        wait_bytes(deep, DEPTH - 1, z_recv)
        total = deep[0].astype(jnp.float32)
        for i in range(1, DEPTH):
            total = total + deep[i].astype(jnp.float32)
        whole[me] = total.astype(jnp.bfloat16)

        for peer in plane:
            pltpu.make_async_remote_copy(
                src_ref=whole.at[me], dst_ref=whole.at[me], send_sem=ag_send, recv_sem=ag_recv.at[own_group],
                device_id=peer, device_id_type=MESH,
            ).start()

    block_of = div(column_rows((TILE, LANES)), RANK)
    result_ref[...] = jnp.zeros_like(result_ref)

    def contract(steps):
        bases, left = [], []
        for step in steps:
            group = group_at(step)
            bases.append(group * GROUP)

            @pl.when(group == own_group)
            def _():
                wait_bytes(whole, GROUP - 1, ag_recv.at[group])

            @pl.when(group != own_group)
            def _():
                wait_bytes(whole, GROUP, ag_recv.at[group])

        for base in bases:
            for i in range(GROUP):
                tile = whole[base + i].astype(jnp.float32)
                left += [jnp.where(block_of == b, tile, 0.0).astype(jnp.bfloat16) for b in range(BLOCKS)]
        result_ref[...] += jnp.dot(
            jnp.concatenate(left, axis=1), rows_of(bases), preferred_element_type=jnp.float32
        )

    def contract_pair(step, carry):
        pair = groups // 2 - step
        contract((2 * pair, 2 * pair + 1))
        return carry

    contract((groups - 1,))
    lax.fori_loop(1, groups // 2 + 1, contract_pair, 0)
    result = result_ref[...]

    half = result[: 2 * RANK] + result[2 * RANK :]
    terms[dp] = half + pltpu.roll(half, RANK, 0)
    replicas = beside + [device(y, x, core, z_other)] + [device(y, xs[step], core, z) for step in (2, 1, 3)]
    for peer in replicas:
        pltpu.make_async_remote_copy(
            src_ref=terms.at[dp], dst_ref=terms.at[dp], send_sem=dp_send, recv_sem=dp_recv,
            device_id=peer, device_id_type=MESH,
        ).start()

    tiles = jnp.concatenate([whole[chunk] for chunk in range(chunks)], axis=1)
    gram = lax.dot_general(tiles, tiles, (((1,), (1,)), ((), ())), preferred_element_type=jnp.float32)
    lower, inverse = inverse_factor(gram)

    def turn(step, carry):
        for i in range(GROUP):
            chunk = step * GROUP + i
            tile = whole[chunk].astype(jnp.float32)
            twice = jnp.concatenate([tile, tile], axis=0)
            left_ref[chunk] = twice.T.astype(jnp.bfloat16)
        return carry

    lax.fori_loop(0, groups, turn, 0)

    wait_bytes(terms, REPLICAS - 1, dp_recv)
    total = terms[0]
    for i in range(1, REPLICAS):
        total = total + terms[i]
    total = total * (1.0 / REPLICAS)
    columns = []
    for j in range(RANK):
        value = total[j : j + 1, :]
        for k in range(j):
            value = value - lower[j, k] * columns[k]
        columns.append(value * inverse[j])
    weights = [None] * RANK
    for j in reversed(range(RANK)):
        value = columns[j]
        for k in range(j + 1, RANK):
            value = value - lower[k, j] * weights[k]
        weights[j] = value * inverse[j]
    for j in range(RANK):
        factor_ref[j : j + 1, :] = columns[j]
    kind = rem(column_rows((TILE, LANES)), RANK)
    spread = jnp.broadcast_to(weights[0], (TILE, LANES))
    for j in range(1, RANK):
        spread = jnp.where(kind == j, weights[j], spread)
    high = spread.astype(jnp.bfloat16).astype(jnp.float32)
    low = spread - high
    for b in range(BLOCKS):
        at = slice(b * LANES, (b + 1) * LANES)
        pair = [jnp.where(block_of == b, part, 0.0) for part in (high, low)]
        right_ref[:, at] = jnp.concatenate(pair, axis=0).astype(jnp.bfloat16)

    @pl.when(owner)
    def _():
        wait_bytes(outgoing, chunks - 1, rs_send)
        wait_bytes(deep, DEPTH - 1, z_send)
        wait_bytes(arrived, PLANE - 1, ag_send)

    @pl.when(jnp.logical_not(owner))
    def _():
        wait_bytes(outgoing, chunks, rs_send)

    wait_bytes(terms, REPLICAS - 1, dp_send)


def residual_kernel(chunks, m_ref, left_ref, right_ref, factor_ref, out_hbm, factor_hbm, out, sem, factor_sem):
    factor_copy = pltpu.make_async_copy(factor_ref, factor_hbm, factor_sem)

    for chunk in range(chunks):
        product = jnp.dot(left_ref[chunk], right_ref[...], preferred_element_type=jnp.float32)
        for b in range(BLOCKS):
            at = slice(b * LANES, (b + 1) * LANES)
            out[chunk, at] = (m_ref[chunk, at] - product[:, at]).astype(jnp.bfloat16)
        pltpu.make_async_copy(out.at[chunk], out_hbm.at[chunk], sem).start()
    factor_copy.start()
    pltpu.make_async_copy(out, out_hbm, sem).wait()
    factor_copy.wait()


def per_device(gradient_part, carried_error, query_basis):
    width = gradient_part.shape[3]
    chunks = gradient_part.shape[1] * gradient_part.shape[2] // CHUNK
    tiled = (chunks, CHUNK, width)
    bf16, f32 = jnp.bfloat16, jnp.float32
    hbm = pl.BlockSpec(memory_space=pltpu.HBM)
    vmem = pl.BlockSpec(memory_space=pltpu.VMEM)
    dma = pltpu.SemaphoreType.DMA
    operands = gradient_part.reshape(tiled), carried_error.reshape(tiled), query_basis.T
    operands = [pltpu.with_memory_space_constraint(operand, pltpu.HBM) for operand in operands]
    merged, left, right, factor = pl.pallas_call(
        functools.partial(factor_kernel, chunks),
        out_shape=(
            pltpu.VMEM(tiled, f32),
            pltpu.VMEM((chunks, LANES, 2 * TILE), bf16),
            pltpu.VMEM((2 * TILE, CHUNK), bf16),
            pltpu.VMEM((RANK, width), f32),
        ),
        in_specs=[hbm, hbm, hbm],
        out_specs=(vmem, vmem, vmem, vmem),
        scratch_shapes=[
            pltpu.VMEM((2, *tiled), bf16),
            pltpu.VMEM(tiled, bf16),
            pltpu.VMEM((RANK, width), f32),
            pltpu.VMEM((chunks, TILE, LANES), bf16),
            pltpu.VMEM((PLANE, TILE, LANES), bf16),
            pltpu.VMEM((DEPTH, TILE, LANES), bf16),
            pltpu.VMEM((chunks, TILE, LANES), bf16),
            pltpu.VMEM((REPLICAS, 2 * RANK, LANES), f32),
            pltpu.VMEM((TILE, LANES), f32),
            dma,
            dma,
            dma((chunks // GROUP,)),
            dma,
        ],
        compiler_params=pltpu.CompilerParams(
            collective_id=0, has_side_effects=True, vmem_limit_bytes=28 << 20
        ),
        name="factor",
    )(*operands)
    returned, factor = pl.pallas_call(
        functools.partial(residual_kernel, chunks),
        out_shape=(pltpu.HBM(tiled, bf16), pltpu.HBM((RANK, width), f32)),
        in_specs=[vmem, vmem, vmem, vmem],
        out_specs=(hbm, hbm),
        scratch_shapes=[pltpu.VMEM(tiled, bf16), dma, dma],
        compiler_params=pltpu.CompilerParams(vmem_limit_bytes=16 << 20),
        name="residual",
    )(merged, left, right, factor)
    return returned.reshape(gradient_part.shape), factor.T


def solution(mesh):
    in_specs = (P("dp", None, None, "head"), P("dp", None, None, "head"), P("head", None))
    out_specs = (P("dp", None, None, "head"), P("head", None))
    return jax.shard_map(
        per_device, mesh=mesh, in_specs=in_specs, out_specs=out_specs, check_vma=False
    )
```

```python
import functools
import itertools

import jax
import jax.numpy as jnp
from jax import lax
from jax.experimental import pallas as pl
from jax.experimental.pallas import tpu as pltpu
from jax.sharding import PartitionSpec as P

MESH = pl.DeviceIdType.MESH
RANK = 4
LANES = 128
BLOCKS = 4
CHUNK = BLOCKS * LANES
TILE = BLOCKS * RANK
GROUP = 3
PLANE = 32
DEPTH = 8
REPLICAS = 8
AHEAD = 3
EARLY = 6


def wrap(a, b):
    return jnp.where(a >= b, a - b, a)


def rem(a, b):
    return lax.rem(a, jnp.int32(b))


def div(a, b):
    return lax.div(a, jnp.int32(b))


def place():
    head, dp = lax.axis_index("head"), lax.axis_index("dp")
    core, z_hi, y = rem(head, 2), rem(div(head, 2), 4), div(head, 8)
    x, z_lo = rem(dp, 4), div(dp, 4)
    return y, x, core, z_hi * 2 + z_lo


def device(y, x, core, z):
    return {"head": (y * 4 + div(z, 2)) * 2 + core, "dp": rem(z, 2) * 4 + x}


def turned(row, column):
    return column + rem(row, 2) * (3 - 2 * column)


def number_of(y, x, core):
    row = wrap(y + 3, 4)
    return (row * 4 + turned(row, x)) * 2 + core


def of_plane(index, z):
    row = div(index, 8)
    return device(wrap(row + 1, 4), turned(row, rem(div(index, 2), 4)), rem(index, 2), z)


def column_rows(shape):
    return lax.broadcasted_iota(jnp.int32, shape, 0)


def inverse_factor(gram):
    rows, columns = column_rows(gram.shape), lax.broadcasted_iota(jnp.int32, gram.shape, 1)

    def entry(j, k):
        picked = (rows - columns == j - k) & ((rows & 3) == j) & ((columns & 3) == k)
        return jnp.sum(jnp.where(picked, gram, 0.0), axis=(0, 1), keepdims=True)

    lower, inverse = {}, []
    for j in range(RANK):
        for k in range(j):
            total = entry(j, k)
            for i in range(k):
                total = total - lower[j, i] * lower[k, i]
            lower[j, k] = total * inverse[k]
        total = entry(j, j)
        for i in range(j):
            total = total - lower[j, i] * lower[j, i]
        inverse.append(1.0 / jnp.sqrt(total))
    return lower, inverse


def factor_kernel(
    chunks, g_hbm, e_hbm, q_hbm, m_ref, left_ref, right_ref, factor_ref,
    ge, rounded, q_ref, outgoing, arrived, deep, whole, terms, result_ref,
    rs_recv, z_recv, ag_recv, dp_recv,
):
    dma = pltpu.SemaphoreType.DMA
    pl.run_scoped(
        functools.partial(
            factor_body, chunks, g_hbm, e_hbm, q_hbm, m_ref, left_ref, right_ref, factor_ref,
            ge, rounded, q_ref, outgoing, arrived, deep, whole, terms, result_ref,
            rs_recv, z_recv, ag_recv, dp_recv,
        ),
        dma((chunks // GROUP - EARLY // 2,)), dma, dma, dma, dma, dma,
    )


def factor_body(
    chunks, g_hbm, e_hbm, q_hbm, m_ref, left_ref, right_ref, factor_ref,
    ge, rounded, q_ref, outgoing, arrived, deep, whole, terms, result_ref,
    rs_recv, z_recv, ag_recv, dp_recv,
    load_sem, q_sem, rs_send, z_send, ag_send, dp_send,
):
    y, x, core, z = place()
    me = number_of(y, x, core)
    dp = rem(z, 2) * 4 + x
    owner = me < chunks
    groups = chunks // GROUP
    own_group = div(me, GROUP)
    centre = wrap(wrap(own_group, groups), groups)

    def group_at(step):
        reach = groups // 2 - div(jnp.int32(step), 2)
        group = centre + reach * (1 - 2 * rem(jnp.int32(step), 2))
        return wrap(jnp.where(group < 0, group + groups, group), groups)

    def loads(step):
        at = pl.ds(group_at(step) * GROUP, GROUP)
        return [
            pltpu.make_async_copy(src.at[at], ge.at[i, at], load_sem.at[max(step // 2, step - EARLY // 2)])
            for i, src in enumerate((g_hbm, e_hbm))
        ]

    q_copy = pltpu.make_async_copy(q_hbm, q_ref, q_sem)
    q_copy.start()
    for step in range(AHEAD):
        for copy in loads(step):
            copy.start()

    ys = [y] + [wrap(y + step, 4) for step in range(1, 4)]
    xs = [x] + [wrap(x + step, 4) for step in range(1, 4)]
    cores = [core, 1 - core]
    zs = [z] + [wrap(z + step, DEPTH) for step in range(1, DEPTH)]
    z_other = div(z, 2) * 2 + 1 - rem(z, 2)
    far_first = lambda steps, sizes: -sum(min(step, size - step) for step, size in zip(steps, sizes))
    plane = sorted(itertools.product(range(4), range(4), range(2)), key=lambda s: far_first(s, (4, 4, 2)))[:-1]
    line = sorted(range(1, DEPTH), key=lambda s: far_first((s,), (DEPTH,)))
    plane = [device(ys[i], xs[j], cores[k], z) for i, j, k in plane]
    line = [device(y, x, core, zs[step]) for step in line]
    beside = [device(y, xs[step], core, z_other) for step in (2, 1, 3)]

    barrier = pltpu.get_barrier_semaphore()
    greeted = plane + line + beside
    for peer in plane:
        pl.semaphore_signal(barrier, inc=1, device_id=peer, device_id_type=MESH)

    q_copy.wait()
    for step in range(AHEAD, groups):
        for copy in loads(step):
            copy.start()
    for peer in line + beside:
        pl.semaphore_signal(barrier, inc=1, device_id=peer, device_id_type=MESH)
    q = q_ref[...]
    high = q.astype(jnp.bfloat16).astype(jnp.float32)
    both = jnp.concatenate([high, q - high], axis=0)
    q_rows = both.astype(jnp.bfloat16)
    upper = column_rows((2 * RANK, LANES)) < RANK

    def rows_of(bases):
        return jnp.concatenate(
            [rounded[pl.ds(base, GROUP)].reshape(GROUP * CHUNK, LANES) for base in bases], axis=0
        )

    def project(first, count, sem):
        bases = [group_at(first + i) * GROUP for i in range(count)]
        done = ge.at[:, pl.ds(0, count * GROUP)]
        pltpu.make_async_copy(done, done, load_sem.at[sem]).wait()
        for base in bases:
            at = pl.ds(base, GROUP)
            rounded[at] = ge[0, at] + ge[1, at]
        product = lax.dot_general(
            q_rows, rows_of(bases), (((1,), (1,)), ((), ())), preferred_element_type=jnp.float32
        )
        total = product + pltpu.roll(product, RANK, 0)
        for i in range(count * GROUP):
            starts = [i * CHUNK + b * LANES for b in range(BLOCKS)]
            pieces = [total[:, start : start + LANES] for start in starts]
            tile = jnp.concatenate(
                [jnp.where(upper, pieces[0], pieces[1]), jnp.where(upper, pieces[2], pieces[3])], axis=0
            )
            outgoing[bases[i // GROUP] + i % GROUP] = tile.astype(jnp.bfloat16)

    def project_pair(pair, carry):
        project(2 * pair, 2, pair)
        return carry

    lax.fori_loop(0, EARLY // 2, project_pair, 0)

    pl.semaphore_wait(barrier, len(greeted))

    def send_terms(step, carry):
        for i in range(GROUP):
            chunk = group_at(step) * GROUP + i

            @pl.when(chunk != me)
            def _():
                pltpu.make_async_remote_copy(
                    src_ref=outgoing.at[chunk], dst_ref=arrived.at[me], send_sem=rs_send, recv_sem=rs_recv,
                    device_id=of_plane(chunk, z), device_id_type=MESH,
                ).start()

        return carry

    lax.fori_loop(0, EARLY, send_terms, 0)
    for step in range(EARLY, groups):
        project(step, 1, step - EARLY // 2)
        send_terms(step, 0)

    @pl.when(owner)
    def _():
        arrived[me] = outgoing[me]

    def merge(chunk, carry):
        m_ref[chunk] = ge[0, chunk].astype(jnp.float32) + ge[1, chunk].astype(jnp.float32)
        return carry

    lax.fori_loop(0, chunks, merge, 0)

    def wait_bytes(ref, count, sem):
        at = ref.at[pl.ds(0, count)]
        pltpu.make_async_copy(at, at, sem).wait()

    @pl.when(owner)
    def _():
        wait_bytes(arrived, PLANE - 1, rs_recv)
        total = arrived[0].astype(jnp.float32)
        for i in range(1, PLANE):
            total = total + arrived[i].astype(jnp.float32)
        deep[z] = total.astype(jnp.bfloat16)
        for peer in line:
            pltpu.make_async_remote_copy(
                src_ref=deep.at[z], dst_ref=deep.at[z], send_sem=z_send, recv_sem=z_recv,
                device_id=peer, device_id_type=MESH,
            ).start()
        wait_bytes(deep, DEPTH - 1, z_recv)
        total = deep[0].astype(jnp.float32)
        for i in range(1, DEPTH):
            total = total + deep[i].astype(jnp.float32)
        whole[me] = total.astype(jnp.bfloat16)

        for peer in plane:
            pltpu.make_async_remote_copy(
                src_ref=whole.at[me], dst_ref=whole.at[me], send_sem=ag_send, recv_sem=ag_recv.at[own_group],
                device_id=peer, device_id_type=MESH,
            ).start()

    block_of = div(column_rows((TILE, LANES)), RANK)
    result_ref[...] = jnp.zeros_like(result_ref)

    def contract(steps):
        bases, left = [], []
        for step in steps:
            group = group_at(step)
            bases.append(group * GROUP)

            @pl.when(group == own_group)
            def _():
                wait_bytes(whole, GROUP - 1, ag_recv.at[group])

            @pl.when(group != own_group)
            def _():
                wait_bytes(whole, GROUP, ag_recv.at[group])

        for base in bases:
            for i in range(GROUP):
                tile = whole[base + i].astype(jnp.float32)
                left += [jnp.where(block_of == b, tile, 0.0).astype(jnp.bfloat16) for b in range(BLOCKS)]
        result_ref[...] += jnp.dot(
            jnp.concatenate(left, axis=1), rows_of(bases), preferred_element_type=jnp.float32
        )

    def contract_pair(step, carry):
        pair = groups // 2 - step
        contract((2 * pair, 2 * pair + 1))
        return carry

    contract((groups - 1,))
    lax.fori_loop(1, groups // 2 + 1, contract_pair, 0)
    result = result_ref[...]

    half = result[: 2 * RANK] + result[2 * RANK :]
    terms[dp] = half + pltpu.roll(half, RANK, 0)
    beside_here = [device(y, xs[step], core, z) for step in (2, 1, 3)]
    replicas = beside + beside_here[:1] + [device(y, x, core, z_other)] + beside_here[1:]
    for peer in replicas:
        pltpu.make_async_remote_copy(
            src_ref=terms.at[dp], dst_ref=terms.at[dp], send_sem=dp_send, recv_sem=dp_recv,
            device_id=peer, device_id_type=MESH,
        ).start()

    tiles = jnp.concatenate([whole[chunk] for chunk in range(chunks)], axis=1)
    gram = lax.dot_general(tiles, tiles, (((1,), (1,)), ((), ())), preferred_element_type=jnp.float32)
    lower, inverse = inverse_factor(gram)

    def turn(step, carry):
        for i in range(GROUP):
            chunk = step * GROUP + i
            tile = whole[chunk].astype(jnp.float32)
            twice = jnp.concatenate([tile, tile], axis=0)
            left_ref[chunk] = twice.T.astype(jnp.bfloat16)
        return carry

    lax.fori_loop(0, groups, turn, 0)

    wait_bytes(terms, REPLICAS - 1, dp_recv)
    total = terms[0]
    for i in range(1, REPLICAS):
        total = total + terms[i]
    total = total * (1.0 / REPLICAS)
    columns = []
    for j in range(RANK):
        value = total[j : j + 1, :]
        for k in range(j):
            value = value - lower[j, k] * columns[k]
        columns.append(value * inverse[j])
    weights = [None] * RANK
    for j in reversed(range(RANK)):
        value = columns[j]
        for k in range(j + 1, RANK):
            value = value - lower[k, j] * weights[k]
        weights[j] = value * inverse[j]
    for j in range(RANK):
        factor_ref[j : j + 1, :] = columns[j]
    kind = rem(column_rows((TILE, LANES)), RANK)
    spread = jnp.broadcast_to(weights[0], (TILE, LANES))
    for j in range(1, RANK):
        spread = jnp.where(kind == j, weights[j], spread)
    high = spread.astype(jnp.bfloat16).astype(jnp.float32)
    low = spread - high
    for b in range(BLOCKS):
        at = slice(b * LANES, (b + 1) * LANES)
        pair = [jnp.where(block_of == b, part, 0.0) for part in (high, low)]
        right_ref[:, at] = jnp.concatenate(pair, axis=0).astype(jnp.bfloat16)

    @pl.when(owner)
    def _():
        wait_bytes(outgoing, chunks - 1, rs_send)
        wait_bytes(deep, DEPTH - 1, z_send)
        wait_bytes(arrived, PLANE - 1, ag_send)

    @pl.when(jnp.logical_not(owner))
    def _():
        wait_bytes(outgoing, chunks, rs_send)

    wait_bytes(terms, REPLICAS - 1, dp_send)


def residual_kernel(chunks, m_ref, left_ref, right_ref, factor_ref, out_hbm, factor_hbm, out, sem, factor_sem):
    factor_copy = pltpu.make_async_copy(factor_ref, factor_hbm, factor_sem)

    for chunk in range(chunks):
        product = jnp.dot(left_ref[chunk], right_ref[...], preferred_element_type=jnp.float32)
        for b in range(BLOCKS):
            at = slice(b * LANES, (b + 1) * LANES)
            out[chunk, at] = (m_ref[chunk, at] - product[:, at]).astype(jnp.bfloat16)
        pltpu.make_async_copy(out.at[chunk], out_hbm.at[chunk], sem).start()
    factor_copy.start()
    pltpu.make_async_copy(out, out_hbm, sem).wait()
    factor_copy.wait()


def per_device(gradient_part, carried_error, query_basis):
    width = gradient_part.shape[3]
    chunks = gradient_part.shape[1] * gradient_part.shape[2] // CHUNK
    tiled = (chunks, CHUNK, width)
    bf16, f32 = jnp.bfloat16, jnp.float32
    hbm = pl.BlockSpec(memory_space=pltpu.HBM)
    vmem = pl.BlockSpec(memory_space=pltpu.VMEM)
    dma = pltpu.SemaphoreType.DMA
    operands = gradient_part.reshape(tiled), carried_error.reshape(tiled), query_basis.T
    operands = [pltpu.with_memory_space_constraint(operand, pltpu.HBM) for operand in operands]
    merged, left, right, factor = pl.pallas_call(
        functools.partial(factor_kernel, chunks),
        out_shape=(
            pltpu.VMEM(tiled, f32),
            pltpu.VMEM((chunks, LANES, 2 * TILE), bf16),
            pltpu.VMEM((2 * TILE, CHUNK), bf16),
            pltpu.VMEM((RANK, width), f32),
        ),
        in_specs=[hbm, hbm, hbm],
        out_specs=(vmem, vmem, vmem, vmem),
        scratch_shapes=[
            pltpu.VMEM((2, *tiled), bf16),
            pltpu.VMEM(tiled, bf16),
            pltpu.VMEM((RANK, width), f32),
            pltpu.VMEM((chunks, TILE, LANES), bf16),
            pltpu.VMEM((PLANE, TILE, LANES), bf16),
            pltpu.VMEM((DEPTH, TILE, LANES), bf16),
            pltpu.VMEM((chunks, TILE, LANES), bf16),
            pltpu.VMEM((REPLICAS, 2 * RANK, LANES), f32),
            pltpu.VMEM((TILE, LANES), f32),
            dma,
            dma,
            dma((chunks // GROUP,)),
            dma,
        ],
        compiler_params=pltpu.CompilerParams(
            collective_id=0, has_side_effects=True, vmem_limit_bytes=28 << 20
        ),
        name="factor",
    )(*operands)
    returned, factor = pl.pallas_call(
        functools.partial(residual_kernel, chunks),
        out_shape=(pltpu.HBM(tiled, bf16), pltpu.HBM((RANK, width), f32)),
        in_specs=[vmem, vmem, vmem, vmem],
        out_specs=(hbm, hbm),
        scratch_shapes=[pltpu.VMEM(tiled, bf16), dma, dma],
        compiler_params=pltpu.CompilerParams(vmem_limit_bytes=16 << 20),
        name="residual",
    )(merged, left, right, factor)
    return returned.reshape(gradient_part.shape), factor.T


def solution(mesh):
    in_specs = (P("dp", None, None, "head"), P("dp", None, None, "head"), P("head", None))
    out_specs = (P("dp", None, None, "head"), P("head", None))
    return jax.shard_map(
        per_device, mesh=mesh, in_specs=in_specs, out_specs=out_specs, check_vma=False
    )
```
